128 devices in a mesh: flow: 8 (over y, core), link: 16 (over x, z).
Axes of the slice: x: 4, y: 4, z: 4, core: 2. Of those that a mesh axis runs over, the one named last changes fastest.
Arguments:
- route_tiles: bfloat16 [1024, 2048, 128], P('flow', 'link'), may hold values from 0 to 1, as said below
- tile_count: int32 [8, 16], P('flow', 'link'), may hold values from 16 to 128, as said below
- tile_flow: int32 [8, 2048], P('flow', 'link'), may hold values from 0 to 1023
- tile_link: int32 [8, 2048], P('flow', 'link'), may hold values from 0 to 511, as said below
- flow_class: int32 [1048576], P('flow'), may hold values from 0 to 255
- class_weight: float32 [256], replicated, may hold values from 0.25 to 4
- access_price: float32 [1048576], P('flow'), may hold values from 0.5 to 4
- capacity: float32 [1048576], P('link'), may hold values from 1 to 8
- init_price: float32 [1048576], P('link'), may hold values from 0.5 to 2
Outputs:
- flow_rate: float32 [1048576], P('flow')
- link_price: float32 [1048576], P('link')
The draws below stay inside these ranges and needn't reach their ends.
Inputs may be any that keep to these rules, and one draw needn't show every extreme that they name: `route_tiles`: entries are 0 or 1. `tile_count`: counts follow 128 divided by 1, 2, 4 or 8; some device uses all 128 slots in every draw. `tile_link`: within one device's slots no link block repeats.
All inputs are finite; a program needn't handle non-finite values.
Results may differ from the reference program's by a relative error of at most 0.0014.
Values may be sent and summed in bfloat16 or wider, within the bound.
No kernel may reach another device: no remote copies, remote signals or barrier semaphores. Data moves between devices by JAX's collectives and lax.ppermute only.
A program may use at most 64 MiB of HBM per device.

```python
import math
import jax
import jax.numpy as jnp
from jax import lax

TILE = 128
CLASSES = 256
FB_G = 1024
LB_G = 512
CAP = 128
ITERS = 2
FLOWS = 1048576
LINKS = 1048576
N_FLOW = 8
N_LINK = 16


def draw_route_tiles(key, part):
    picks = jax.random.randint(key, (N_FLOW * CAP, N_LINK * TILE, TILE), 0, 16)
    return (picks == 0).astype(jnp.float32).astype(jnp.bfloat16)


def draw_tile_count(key, part):
    powers = jax.random.randint(key, (N_FLOW * N_LINK,), 0, 4)
    counts = CAP // jnp.power(2, powers).astype(jnp.int32)
    picked = jax.random.randint(jax.random.fold_in(key, 1), (), 0, N_FLOW * N_LINK)
    counts = jnp.where(jnp.arange(N_FLOW * N_LINK) == picked, CAP, counts)
    return counts.reshape(N_FLOW, N_LINK).astype(jnp.int32)


def draw_tile_link(key, part):
    keys = jax.random.split(key, N_FLOW * N_LINK)
    picks = jax.vmap(lambda k: jax.random.permutation(k, LB_G)[:CAP])(keys)
    return picks.reshape(N_FLOW, N_LINK * CAP).astype(jnp.int32)


def with_ends(array, rng, low, largest):
    shape = array.shape
    index_at = [jax.random.randint(jax.random.fold_in(rng, axis), (), 0, shape[axis]) for axis in range(len(shape))]
    array = array.at[tuple(index_at)].set(low)
    longest = shape.index(max(shape))
    index_at[longest] = (index_at[longest] + 1) % shape[longest]
    return array.at[tuple(index_at)].set(largest)


def shard_levels(own_key, dims, cuts, low, high):
    gain, own = 1.0, jax.random.fold_in(own_key, 6)
    for axis_at, parts in cuts:
        steps = jnp.exp(jax.random.uniform(jax.random.fold_in(own, axis_at), (parts,), jnp.float32, low / len(cuts), high / len(cuts)))
        gain = gain * jnp.repeat(steps, dims[axis_at] // parts).reshape([-1 if axis == axis_at else 1 for axis in range(len(dims))])
    return gain


def setup_inputs(seed: int = 0) -> dict:
    streams_of = jax.random.split(jax.random.key(seed), 10)
    return {
        "route_tiles": draw_route_tiles(jax.random.fold_in(streams_of[9], 71), 0),
        "tile_count": draw_tile_count(jax.random.fold_in(streams_of[9], 71), 0),
        "tile_flow": with_ends(jax.random.randint(streams_of[2], (N_FLOW, N_LINK * CAP), 0, FB_G), jax.random.fold_in(streams_of[2], 1), 0, FB_G - 1).astype(jnp.int32),
        "tile_link": draw_tile_link(jax.random.fold_in(streams_of[9], 71), 0),
        "flow_class": with_ends(jax.random.randint(streams_of[4], (FLOWS,), 0, CLASSES), jax.random.fold_in(streams_of[4], 1), 0, CLASSES - 1).astype(jnp.int32),
        "class_weight": jnp.clip(jnp.exp(jax.random.uniform(streams_of[5], (CLASSES,), jnp.float32, math.log(0.25), math.log(4.0))), 0.25, 4.0),
        "access_price": jnp.clip(jnp.exp(math.log(4.0) - 2.0794415 * jax.random.uniform(streams_of[6], (FLOWS,), jnp.float32) ** shard_levels(streams_of[6], (FLOWS,), ((0, 8),), -0.2, 0.2)), 0.5, 4.0),
        "capacity": jnp.clip(jnp.exp(math.log(8.0) - 2.0794415 * jax.random.uniform(streams_of[7], (LINKS,), jnp.float32) ** shard_levels(streams_of[7], (LINKS,), ((0, 16),), -0.2, 0.2)), 1.0, 8.0),
        "init_price": jnp.clip(jnp.exp(math.log(2.0) - 1.3862944 * jax.random.uniform(streams_of[8], (LINKS,), jnp.float32) ** shard_levels(streams_of[8], (LINKS,), ((0, 16),), -0.2, 0.2)), 0.5, 2.0),
    }


step_size = 0.5


def reference(route_tiles, tile_count, tile_flow, tile_link, flow_class, class_weight, access_price, capacity, init_price):
    devices_all = N_FLOW * N_LINK
    tiles = route_tiles.reshape(N_FLOW, CAP, N_LINK, TILE, TILE).transpose(0, 2, 1, 3, 4).reshape(devices_all, CAP, TILE, TILE)
    flow_idx = tile_flow.reshape(N_FLOW, N_LINK, CAP) + (jnp.arange(N_FLOW, dtype=jnp.int32) * FB_G)[:, None, None]
    link_idx = tile_link.reshape(N_FLOW, N_LINK, CAP) + (jnp.arange(N_LINK, dtype=jnp.int32) * LB_G)[None, :, None]
    flow_idx = flow_idx.reshape(devices_all, CAP).astype(jnp.int32)
    link_idx = link_idx.reshape(devices_all, CAP).astype(jnp.int32)
    valid = (jnp.arange(CAP, dtype=jnp.int32)[None, :] < tile_count.reshape(devices_all, 1)).astype(jnp.float32)
    weight = class_weight[flow_class].reshape(N_FLOW * FB_G, TILE)
    access = access_price.reshape(N_FLOW * FB_G, TILE)
    link_cap = capacity.reshape(N_LINK * LB_G, TILE)
    price = init_price.reshape(N_LINK * LB_G, TILE)

    def route_sums(price_b):
        def one(total, item):
            tile_set, fl, li, mask = item
            gathered = price_b[li].astype(jnp.float32)
            term = jnp.einsum("sab,sa->sb", tile_set.astype(jnp.float32), gathered) * mask[:, None]
            return total.at[fl].add(term), None
        start = jnp.zeros((N_FLOW * FB_G, TILE), jnp.float32)
        return lax.scan(one, start, (tiles, flow_idx, link_idx, valid))[0]

    def load_sums(rate_b):
        def one(total, item):
            tile_set, fl, li, mask = item
            gathered = rate_b[fl].astype(jnp.float32)
            term = jnp.einsum("sab,sb->sa", tile_set.astype(jnp.float32), gathered) * mask[:, None]
            return total.at[li].add(term), None
        start = jnp.zeros((N_LINK * LB_G, TILE), jnp.float32)
        return lax.scan(one, start, (tiles, flow_idx, link_idx, valid))[0]

    rate = jnp.zeros_like(weight)
    for step in range(ITERS):
        route_sum = route_sums(price.astype(jnp.bfloat16))
        rate = weight / (access + route_sum)
        load = load_sums(rate.astype(jnp.bfloat16))
        price = price * jnp.exp(step_size * (load / link_cap - 1.0))
    return rate.reshape(-1), price.reshape(-1)
```

```python
import jax
import jax.numpy as jnp
from jax import lax
from jax.experimental import pallas as pl
from jax.experimental.pallas import tpu as pltpu
from jax.sharding import PartitionSpec as P

ITERS = 2
step_size = 0.5


f32 = jnp.float32
bf16 = jnp.bfloat16

T = 128
S = 128
PAD = 8
GROUP = 16
CHUNKS = S // GROUP

ANY = pl.BlockSpec(memory_space=pl.ANY)
VM = pl.BlockSpec(memory_space=pltpu.VMEM)
SM = pl.BlockSpec(memory_space=pltpu.SMEM)

TILE_SCRATCH = [
    pltpu.VMEM((S, T, T), bf16),
    pltpu.SemaphoreType.DMA((CHUNKS,)),
    pltpu.VMEM((S, T), bf16),
]


def dot(a, b):
    return lax.dot_general(a, b, (((1,), (0,)), ((), ())), preferred_element_type=f32)


def dot_t(a, b):
    return lax.dot_general(a, b, (((1,), (1,)), ((), ())), preferred_element_type=f32)


def used_index(index_row, count, unused=-1.0):
    slot = lax.broadcasted_iota(jnp.int32, index_row.shape, 1)
    return jnp.where(slot < count, index_row.astype(f32), unused)


def own_column(index_row, count):
    return jnp.broadcast_to(used_index(index_row, count, -2.0), (S, S)).T


def match(column, row):
    return jnp.where(column == row, 1.0, 0.0).astype(bf16)


def matched_sums(columns, blocks):
    sums = [jnp.zeros((S, T), f32) for _ in columns]
    for ref in blocks:
        for k in range(ref.shape[0]):
            terms = ref[k, :S, :]
            row = ref[k, S : S + 1, :]
            high = terms.astype(bf16)
            low = (terms - high.astype(f32)).astype(bf16)
            both = jnp.concatenate([high, low], axis=0)
            for at, column in enumerate(columns):
                hit = match(column, row)
                sums[at] += dot(jnp.concatenate([hit, hit], axis=1), both)
    return sums


def tile_copy(tiles, buf, sems, g):
    return pltpu.make_async_copy(tiles.at[pl.ds(g * GROUP, GROUP)], buf.at[pl.ds(g * GROUP, GROUP)], sems.at[g])


def start_tiles(tiles, buf, sems):
    for g in range(CHUNKS):
        tile_copy(tiles, buf, sems, g).start()


def route_terms(tiles, buf, sems, picked, out):
    lane_slot = lax.broadcasted_iota(jnp.int32, (GROUP, GROUP * T), 1) // T
    slot = lax.broadcasted_iota(jnp.int32, (GROUP, GROUP * T), 0)
    own = lane_slot == slot

    def body(g, carry):
        tile_copy(tiles, buf, sems, g).wait()
        rows = picked[pl.ds(g * GROUP, GROUP), :]
        spread = jnp.concatenate([rows] * GROUP, axis=1)
        spread = jnp.where(own, spread.astype(f32), 0.0).astype(bf16)
        group = buf[pl.ds(g * GROUP, GROUP)].reshape(GROUP * T, T)
        out[pl.ds(g * GROUP, GROUP), :] = dot(spread, group)
        return carry

    lax.fori_loop(0, CHUNKS, body, 0)


def load_terms(tiles, buf, sems, sent, out):
    slot = lax.broadcasted_iota(jnp.int32, (GROUP, T), 0)

    def body(g, carry):
        tile_copy(tiles, buf, sems, g).wait()
        rows = sent[pl.ds(g * GROUP, GROUP), :]
        group = buf[pl.ds(g * GROUP, GROUP)].reshape(GROUP * T, T)
        wide = dot_t(rows, group)
        acc = jnp.zeros((GROUP, T), f32)
        for i in range(GROUP):
            acc = jnp.where(slot == i, wide[:, i * T : (i + 1) * T], acc)
        out[pl.ds(g * GROUP, GROUP), :] = acc
        return carry

    lax.fori_loop(0, CHUNKS, body, 0)


def put_index(out, row):
    out[S : S + PAD, :] = jnp.broadcast_to(row, (PAD, T))


def first_route_kernel(count, flow_row, link_row, price, tiles, out, buf, sems, picked):
    start_tiles(tiles, buf, sems)
    column = own_column(link_row[...], count[0, 0])
    got = jnp.zeros((S, T), f32)
    for c in range(price.shape[0] // T):
        at = lax.broadcasted_iota(jnp.int32, (S, T), 1).astype(f32) + float(c * T)
        got += dot(match(column, at), price[c * T : (c + 1) * T, :].astype(bf16))
    picked[...] = got.astype(bf16)
    route_terms(tiles, buf, sems, picked, out)
    put_index(out, used_index(flow_row[...], count[0, 0]))


def load_kernel(count, flow_row, link_row, own, tiles, *rest):
    blocks, (out, buf, sems, sent) = rest[:-4], rest[-4:]
    start_tiles(tiles, buf, sems)
    column = own_column(flow_row[...], count[0, 0])
    (route_sum,) = matched_sums([column], blocks)
    sent[...] = (own[0] / (own[1] + route_sum)).astype(bf16)
    load_terms(tiles, buf, sems, sent, out)
    put_index(out, used_index(link_row[...], count[0, 0]))


def route_kernel(count, flow_row, link_row, own, tiles, *rest):
    blocks, (out, buf, sems, picked) = rest[:-4], rest[-4:]
    start_tiles(tiles, buf, sems)
    column = own_column(link_row[...], count[0, 0])
    (load,) = matched_sums([column], blocks)
    picked[...] = (own[2] * jnp.exp(step_size * (load / own[3] - 1.0))).astype(bf16)
    route_terms(tiles, buf, sems, picked, out)
    put_index(out, used_index(flow_row[...], count[0, 0]))


def block_columns(n):
    at = lax.broadcasted_iota(jnp.int32, (S, T), 0).astype(f32)
    return [at + float(c * T) for c in range(n // T)]


def rate_kernel(weight, access, *rest):
    blocks, out = rest[:-1], rest[-1]
    for c, total in enumerate(matched_sums(block_columns(out.shape[0]), blocks)):
        rows = slice(c * T, (c + 1) * T)
        out[rows, :] = weight[rows, :] / (access[rows, :] + total)


def price_kernel(price, capacity, *rest):
    blocks, out = rest[:-1], rest[-1]
    for c, total in enumerate(matched_sums(block_columns(out.shape[0]), blocks)):
        rows = slice(c * T, (c + 1) * T)
        out[rows, :] = price[rows, :] * jnp.exp(step_size * (total / capacity[rows, :] - 1.0))


def prepare_kernel(flow_at, link_at, flow_class, table, access, price, capacity, weight, own):
    low = jnp.broadcast_to(table[0:1, :], (8, T))
    high = jnp.broadcast_to(table[1:2, :], (8, T))

    def look(r, carry):
        rows = pl.ds(pl.multiple_of(r * 8, 8), 8)
        which = flow_class[rows, :]
        lane = which & (T - 1)
        from_low = jnp.take_along_axis(low, lane, axis=1)
        from_high = jnp.take_along_axis(high, lane, axis=1)
        weight[rows, :] = jnp.where(which < T, from_low, from_high)
        return carry

    lax.fori_loop(0, flow_class.shape[0] // 8, look, 0, unroll=8)

    def pick(s, carry):
        f = flow_at[0, s]
        l = link_at[0, s]
        own[0, pl.ds(s, 1), :] = weight[pl.ds(f, 1), :]
        own[1, pl.ds(s, 1), :] = access[pl.ds(f, 1), :]
        own[2, pl.ds(s, 1), :] = price[pl.ds(l, 1), :]
        own[3, pl.ds(s, 1), :] = capacity[pl.ds(l, 1), :]
        return carry

    lax.fori_loop(0, S, pick, 0, unroll=8)


def shifts():
    def device(y, core, x, z):
        return ((y % 4) * 2 + core) * 16 + (x % 4) * 4 + z % 4

    every = [(y, c, x, z) for y in range(4) for c in range(2) for x in range(4) for z in range(4)]

    def moved(f):
        return [(device(*p), device(*f(*p))) for p in every]

    order = (1, 3, 2)
    first = [moved(lambda y, c, x, z, d=d: (y, c, x + d, z) if c == 0 else (y, c, x, z + d)) for d in order]
    second = [moved(lambda y, c, x, z, d=d: (y, c, x, z + d) if c == 0 else (y, c, x + d, z)) for d in order]
    along_y = [moved(lambda y, c, x, z, d=d: (y + d, c, x, z)) for d in order]
    partner = moved(lambda y, c, x, z: (y, 1 - c, x, z))
    return first, second, along_y, partner


FIRST, SECOND, ALONG_Y, PARTNER = shifts()


def send(x, perm):
    return lax.ppermute(x, ("flow", "link"), perm)


def gather_link(x):
    near = jnp.stack([x] + [send(x, p) for p in FIRST])
    return [near] + [send(near, p) for p in SECOND]


def gather_flow(x):
    near = jnp.stack([x] + [send(x, p) for p in ALONG_Y])
    return [near, send(near, PARTNER)]


def on_device(
    route_tiles,
    tile_count,
    tile_flow,
    tile_link,
    flow_class,
    class_weight,
    access_price,
    capacity,
    init_price,
):
    flow_blocks = access_price.shape[0] // T
    link_blocks = capacity.shape[0] // T
    cap = capacity.reshape(link_blocks, T)
    price = init_price.reshape(link_blocks, T)
    access = access_price.reshape(flow_blocks, T)
    payload = jax.ShapeDtypeStruct((S + PAD, T), f32)

    def tile_call(body, name, own, blocks):
        return pl.pallas_call(
            body,
            out_shape=payload,
            in_specs=[SM, VM, VM, VM, ANY] + [VM] * len(blocks),
            out_specs=VM,
            scratch_shapes=TILE_SCRATCH,
            name=name,
        )(tile_count, tile_flow, tile_link, own, route_tiles, *blocks)

    def full_call(body, name, a, b, blocks):
        return pl.pallas_call(
            body,
            out_shape=jax.ShapeDtypeStruct(a.shape, f32),
            in_specs=[VM] * (2 + len(blocks)),
            out_specs=VM,
            name=name,
        )(a, b, *blocks)

    route_one = tile_call(first_route_kernel, "first_route", price, [])
    weight, own = pl.pallas_call(
        prepare_kernel,
        out_shape=(
            jax.ShapeDtypeStruct((flow_blocks, T), f32),
            jax.ShapeDtypeStruct((4, S, T), f32),
        ),
        in_specs=[SM, SM] + [VM] * 5,
        out_specs=(VM, VM),
        name="prepare",
    )(tile_flow, tile_link, flow_class.reshape(flow_blocks, T), class_weight.reshape(2, T), access, price, cap)

    routes = gather_link(route_one)
    loads = gather_flow(tile_call(load_kernel, "load_one", own, routes))
    price_one = full_call(price_kernel, "price_one", price, cap, loads)
    routes = gather_link(tile_call(route_kernel, "route_two", own, loads))
    rate = full_call(rate_kernel, "rate_two", weight, access, routes)
    loads = gather_flow(tile_call(load_kernel, "load_two", own, routes))
    price_two = full_call(price_kernel, "price_two", price_one, cap, loads)
    return (rate.reshape(-1), price_two.reshape(-1))


def solution(mesh):
    return jax.shard_map(
        on_device,
        mesh=mesh,
        in_specs=(
            P("flow", "link", None),
            P("flow", "link"),
            P("flow", "link"),
            P("flow", "link"),
            P("flow"),
            P(),
            P("flow"),
            P("link"),
            P("link"),
        ),
        out_specs=(P("flow"), P("link")),
        check_vma=False,
    )
```

```python
import jax
import jax.numpy as jnp
from jax import lax
from jax.experimental import pallas as pl
from jax.experimental.pallas import tpu as pltpu
from jax.sharding import PartitionSpec as P


step_size = 0.5


f32 = jnp.float32
bf16 = jnp.bfloat16

T = 128
S = 128
HALF = S // 2
PAYLOAD = HALF + 8
INDEX = HALF
EXPONENT = HALF + 1
GROUP = 16
CHUNKS = S // GROUP

SM = pl.BlockSpec(memory_space=pltpu.SMEM)
HB = pl.BlockSpec(memory_space=pltpu.HBM)
VM = pl.BlockSpec(memory_space=pltpu.VMEM)
PARAMS = pltpu.CompilerParams(vmem_limit_bytes=16 << 20)


def in_vmem(x):
    return pltpu.with_memory_space_constraint(x, pltpu.VMEM)


def in_hbm(x):
    return pltpu.with_memory_space_constraint(x, pltpu.HBM)


def dot(a, b):
    return lax.dot_general(a, b, (((1,), (0,)), ((), ())), preferred_element_type=f32)


def dot_t(a, b):
    return lax.dot_general(a, b, (((1,), (1,)), ((), ())), preferred_element_type=f32)


def used_index(index_row, count, unused=-1):
    slot = lax.broadcasted_iota(jnp.int32, index_row.shape, 1)
    return jnp.where(slot < count, index_row, unused)


def own_column(index_row, count):
    row = used_index(index_row, count, -2).astype(f32)
    return jnp.broadcast_to(row, (S, S)).T.astype(jnp.int32)


def put_payload(out, terms, index_row):
    largest = jnp.max(terms, axis=1, keepdims=True)
    exponent = jnp.floor(jnp.log(jnp.maximum(largest, 1e-30)) * 1.4426950408889634) + 1.0
    scale = jnp.exp2(16.0 - exponent)
    coded = jnp.minimum(jnp.round(terms * scale), 65535.0).astype(jnp.int32)
    out[:HALF, :] = coded[:HALF, :] | (coded[HALF:, :] << 16)
    out[INDEX:EXPONENT, :] = index_row
    exponent_row = jnp.broadcast_to(exponent, (S, S)).T[:1, :].astype(jnp.int32)
    out[EXPONENT : EXPONENT + 1, :] = exponent_row


def decoded(words):
    top = lax.shift_right_logical(words, 16)
    high = jnp.concatenate([words & 0xFF00, top & 0xFF00], axis=0)
    low = jnp.concatenate([words & 0xFF, top & 0xFF], axis=0)
    return jnp.concatenate([high.astype(f32).astype(bf16), low.astype(f32).astype(bf16)], axis=1)


def matched_sum(column, blocks, codes):
    hits = []
    for ref in blocks:
        for k in range(ref.shape[0]):
            scale = jnp.exp2((ref[k, EXPONENT : EXPONENT + 1, :] - 16).astype(f32))
            hits.append(jnp.where(column == ref[k, INDEX:EXPONENT, :], scale, 0.0).astype(bf16))
    both = dot(jnp.concatenate(hits, axis=1), codes)
    return both[:, :T] + both[:, T:]


def decode(blocks):
    return jnp.concatenate([decoded(ref[k, :HALF, :]) for ref in blocks for k in range(ref.shape[0])], axis=0)


def own_slots():
    lane_slot = lax.broadcasted_iota(jnp.int32, (GROUP, GROUP * T), 1) // T
    return lane_slot == lax.broadcasted_iota(jnp.int32, (GROUP, GROUP * T), 0)


def spread(rows, own):
    return jnp.where(own, jnp.concatenate([rows] * GROUP, axis=1).astype(f32), 0.0).astype(bf16)


def route_terms(tiles, ready, picked, out):
    own = own_slots()

    def body(g, carry):
        ready(g)
        rows = pl.ds(g * GROUP, GROUP)
        out[rows, :] = dot(spread(picked[rows, :], own), tiles[rows].reshape(GROUP * T, T))
        return carry

    lax.fori_loop(0, CHUNKS, body, 0)


def load_terms(tiles, sent, out):
    own = own_slots()

    def body(g, carry):
        rows = pl.ds(g * GROUP, GROUP)
        wide = jnp.concatenate([tiles[g * GROUP + i] for i in range(GROUP)], axis=1)
        out[rows, :] = dot_t(spread(sent[rows, :], own), wide)
        return carry

    lax.fori_loop(0, CHUNKS, body, 0)


def first_route_kernel(
    count, flow_in, link_in, price_in, tiles, out, kept, index, sems, more, flow_row, link_row, price, picked, terms
):
    small = [
        pltpu.make_async_copy(a, b, more.at[i])
        for i, (a, b) in enumerate(((flow_in, flow_row), (link_in, link_row), (price_in, price)))
    ]

    def copy(g):
        rows = pl.ds(g * GROUP, GROUP)
        return pltpu.make_async_copy(tiles.at[rows], kept.at[rows], sems.at[g])

    for c in small:
        c.start()
    for g in range(CHUNKS):
        copy(g).start()
    for c in small:
        c.wait()
    used = count[0, 0]
    flow_used = used_index(flow_row[...], used)
    index[:S, :] = own_column(flow_row[...], used)
    column = own_column(link_row[...], used)
    index[S : 2 * S, :] = column
    index[2 * S : 2 * S + 1, :] = flow_used
    index[2 * S + 1 : 2 * S + 2, :] = used_index(link_row[...], used)
    at = lax.broadcasted_iota(jnp.int32, (S, T), 1)
    hits = [jnp.where(column == at + c * T, 1.0, 0.0).astype(bf16) for c in range(price.shape[0] // T)]
    picked[...] = dot(jnp.concatenate(hits, axis=1), price[...].astype(bf16)).astype(bf16)
    route_terms(kept, lambda g: copy(g).wait(), picked, terms)
    put_payload(out, terms[...], flow_used)


def load_kernel(index, own, tiles, *rest):
    blocks, (out, sent, terms) = rest[:-3], rest[-3:]
    route_sum = matched_sum(index[:S, :], blocks, decode(blocks))
    sent[...] = (own[0] / (own[1] + route_sum)).astype(bf16)
    load_terms(tiles, sent, terms)
    put_payload(out, terms[...], index[2 * S + 1 : 2 * S + 2, :])


def route_kernel(index, own, tiles, *rest):
    blocks, (out, picked, terms) = rest[:-3], rest[-3:]
    load = matched_sum(index[S : 2 * S, :], blocks, decode(blocks))
    picked[...] = (own[2] * jnp.exp(step_size * (load / own[3] - 1.0))).astype(bf16)
    route_terms(tiles, lambda g: None, picked, terms)
    put_payload(out, terms[...], index[2 * S : 2 * S + 1, :])


def rate_kernel(weight, access, *rest):
    blocks, (out, code) = rest[:-2], rest[-2:]
    code[...] = decode(blocks)

    def body(c, carry):
        column = lax.broadcasted_iota(jnp.int32, (S, T), 0) + c * T
        total = matched_sum(column, blocks, code[...])
        rows = pl.ds(pl.multiple_of(c * T, T), T)
        out[rows, :] = weight[rows, :] / (access[rows, :] + total)
        return carry

    lax.fori_loop(0, out.shape[0] // T, body, 0)


def price_kernel(price, capacity, *rest):
    blocks, (out, code) = rest[:-2], rest[-2:]
    code[...] = decode(blocks)

    def body(c, carry):
        column = lax.broadcasted_iota(jnp.int32, (S, T), 0) + c * T
        total = matched_sum(column, blocks, code[...])
        rows = pl.ds(pl.multiple_of(c * T, T), T)
        out[rows, :] = price[rows, :] * jnp.exp(step_size * (total / capacity[rows, :] - 1.0))
        return carry

    lax.fori_loop(0, out.shape[0] // T, body, 0)


def prepare_kernel(flow_in, link_in, flow_class, table, access, price, capacity, weight, own, sems, flow_at, link_at):
    small = [pltpu.make_async_copy(flow_in, flow_at, sems.at[0]), pltpu.make_async_copy(link_in, link_at, sems.at[1])]
    for c in small:
        c.start()
    low = jnp.broadcast_to(table[0:1, :], (8, T))
    high = jnp.broadcast_to(table[1:2, :], (8, T))

    def look(r, carry):
        rows = pl.ds(pl.multiple_of(r * 8, 8), 8)
        which = flow_class[rows, :]
        lane = which & (T - 1)
        from_low = jnp.take_along_axis(low, lane, axis=1)
        from_high = jnp.take_along_axis(high, lane, axis=1)
        weight[rows, :] = jnp.where(which < T, from_low, from_high)
        return carry

    lax.fori_loop(0, flow_class.shape[0] // 8, look, 0, unroll=8)

    for c in small:
        c.wait()

    def pick(s, carry):
        f = flow_at[0, s]
        l = link_at[0, s]
        own[0, pl.ds(s, 1), :] = weight[pl.ds(f, 1), :]
        own[1, pl.ds(s, 1), :] = access[pl.ds(f, 1), :]
        own[2, pl.ds(s, 1), :] = price[pl.ds(l, 1), :]
        own[3, pl.ds(s, 1), :] = capacity[pl.ds(l, 1), :]
        return carry

    lax.fori_loop(0, S, pick, 0, unroll=8)


def shifts():
    def device(y, core, x, z):
        return ((y % 4) * 2 + core) * 16 + (x % 4) * 4 + z % 4

    every = [(y, c, x, z) for y in range(4) for c in range(2) for x in range(4) for z in range(4)]

    def moved(f):
        return [(device(*p), device(*f(*p))) for p in every]

    order = (1, 3, 2)
    first = [moved(lambda y, c, x, z, d=d: (y, c, x + d, z) if c == 0 else (y, c, x, z + d)) for d in order]
    second = [moved(lambda y, c, x, z, d=d: (y, c, x, z + d) if c == 0 else (y, c, x + d, z)) for d in order]
    along_y = [moved(lambda y, c, x, z, d=d: (y + d, c, x, z)) for d in order]
    partner = moved(lambda y, c, x, z: (y, 1 - c, x, z))
    return first, second, along_y, partner


FIRST, SECOND, ALONG_Y, PARTNER = shifts()


def send(x, perm):
    return lax.ppermute(x, ("flow", "link"), perm)


def gather_link(x):
    near = jnp.stack([x] + [send(x, p) for p in FIRST])
    far = []
    for p in SECOND:
        far.append(send(near, p))
    return [near] + far


def gather_flow(x):
    near = [x]
    for p in ALONG_Y:
        near.append(send(x, p))
    near = jnp.stack(near)
    return [near, send(near, PARTNER)]


def on_device(
    route_tiles,
    tile_count,
    tile_flow,
    tile_link,
    flow_class,
    class_weight,
    access_price,
    capacity,
    init_price,
):
    flow_blocks = access_price.shape[0] // T
    link_blocks = capacity.shape[0] // T
    cap = capacity.reshape(link_blocks, T)
    price = init_price.reshape(link_blocks, T)
    access = access_price.reshape(flow_blocks, T)
    payload = pltpu.VMEM((PAYLOAD, T), jnp.int32)

    def tile_call(body, own, tiles, blocks):
        return pl.pallas_call(
            body,
            out_shape=payload,
            in_specs=[VM] * (3 + len(blocks)),
            out_specs=VM,
            scratch_shapes=[pltpu.VMEM((S, T), bf16), pltpu.VMEM((S, T), f32)],
            compiler_params=PARAMS,
        )(in_vmem(index), in_vmem(own), in_vmem(tiles), *[in_vmem(x) for x in blocks])

    def full_call(body, a, b, blocks):
        pieces = sum(x.shape[0] for x in blocks)
        return pl.pallas_call(
            body,
            out_shape=jax.ShapeDtypeStruct(a.shape, f32),
            in_specs=[VM] * (2 + len(blocks)),
            out_specs=VM,
            scratch_shapes=[pltpu.VMEM((pieces * S, 2 * T), bf16)],
            compiler_params=PARAMS,
        )(a, b, *[in_vmem(x) for x in blocks])

    route_one, tiles, index = pl.pallas_call(
        first_route_kernel,
        out_shape=(payload, pltpu.VMEM((S, T, T), bf16), pltpu.VMEM((2 * S + 8, T), jnp.int32)),
        in_specs=[SM] + [HB] * 4,
        out_specs=(VM, VM, VM),
        scratch_shapes=[
            pltpu.SemaphoreType.DMA((CHUNKS,)),
            pltpu.SemaphoreType.DMA((3,)),
            pltpu.VMEM((1, S), jnp.int32),
            pltpu.VMEM((1, S), jnp.int32),
            pltpu.VMEM(price.shape, f32),
            pltpu.VMEM((S, T), bf16),
            pltpu.VMEM((S, T), f32),
        ],
        compiler_params=PARAMS,
        name="first_route",
    )(tile_count, *[in_hbm(x) for x in (tile_flow, tile_link, price, route_tiles)])
    weight, own = pl.pallas_call(
        prepare_kernel,
        out_shape=(pltpu.VMEM((flow_blocks, T), f32), pltpu.VMEM((4, S, T), f32)),
        in_specs=[HB, HB] + [VM] * 5,
        out_specs=(VM, VM),
        scratch_shapes=[pltpu.SemaphoreType.DMA((2,)), pltpu.SMEM((1, S), jnp.int32), pltpu.SMEM((1, S), jnp.int32)],
        compiler_params=PARAMS,
        name="prepare",
    )(in_hbm(tile_flow), in_hbm(tile_link), flow_class.reshape(flow_blocks, T), class_weight.reshape(2, T), access, price, cap)

    routes = gather_link(route_one)
    loads = gather_flow(tile_call(load_kernel, own, tiles, routes))
    price_one = full_call(price_kernel, price, cap, loads)
    routes = gather_link(tile_call(route_kernel, own, tiles, loads))
    rate = full_call(rate_kernel, weight, access, routes)
    loads = gather_flow(tile_call(load_kernel, own, tiles, routes))
    price_two = full_call(price_kernel, price_one, cap, loads)
    return (rate.reshape(-1), price_two.reshape(-1))


def solution(mesh):
    return jax.shard_map(
        on_device,
        mesh=mesh,
        in_specs=(
            P("flow", "link", None),
            P("flow", "link"),
            P("flow", "link"),
            P("flow", "link"),
            P("flow"),
            P(),
            P("flow"),
            P("link"),
            P("link"),
        ),
        out_specs=(P("flow"), P("link")),
        check_vma=False,
    )
```

```python
import jax
import jax.numpy as jnp
from jax import lax
from jax.experimental import pallas as pl
from jax.experimental.pallas import tpu as pltpu
from jax.sharding import PartitionSpec as P


step_size = 0.5


f32 = jnp.float32
bf16 = jnp.bfloat16

T = 128
S = 128
HALF = S // 2
PAYLOAD = HALF + 8
INDEX = HALF
EXPONENT = HALF + 1
GROUP = 16
CHUNKS = S // GROUP
FETCH = 32

SM = pl.BlockSpec(memory_space=pltpu.SMEM)
HB = pl.BlockSpec(memory_space=pltpu.HBM)
VM = pl.BlockSpec(memory_space=pltpu.VMEM)
PARAMS = pltpu.CompilerParams(vmem_limit_bytes=16 << 20)


def in_vmem(x):
    return pltpu.with_memory_space_constraint(x, pltpu.VMEM)


def in_hbm(x):
    return pltpu.with_memory_space_constraint(x, pltpu.HBM)


def dot(a, b):
    return lax.dot_general(a, b, (((1,), (0,)), ((), ())), preferred_element_type=f32)


def used_index(index_row, count, unused=-1):
    slot = lax.broadcasted_iota(jnp.int32, index_row.shape, 1)
    return jnp.where(slot < count, index_row, unused)


def own_column(index_row, count):
    row = used_index(index_row, count, -2).astype(f32)
    return jnp.broadcast_to(row, (S, S)).T.astype(jnp.int32)


def put_payload(out, terms, index_row):
    largest = jnp.max(terms, axis=1, keepdims=True)
    exponent = jnp.floor(jnp.log(jnp.maximum(largest, 1e-30)) * 1.4426950408889634) + 1.0
    scale = jnp.exp2(16.0 - exponent)
    coded = jnp.minimum(jnp.round(terms * scale), 65535.0).astype(jnp.int32)
    out[:HALF, :] = coded[:HALF, :] | (coded[HALF:, :] << 16)
    out[INDEX:EXPONENT, :] = index_row
    exponent_row = jnp.broadcast_to(exponent, (S, S)).T[:1, :].astype(jnp.int32)
    out[EXPONENT : EXPONENT + 1, :] = exponent_row


def decoded(words):
    top = lax.shift_right_logical(words, 16)
    high = jnp.concatenate([words & 0xFF00, top & 0xFF00], axis=0)
    low = jnp.concatenate([words & 0xFF, top & 0xFF], axis=0)
    return jnp.concatenate([high.astype(f32).astype(bf16), low.astype(f32).astype(bf16)], axis=1)


def matched_sum(column, blocks, codes):
    hits = []
    for ref in blocks:
        for k in range(ref.shape[0]):
            scale = jnp.exp2((ref[k, EXPONENT : EXPONENT + 1, :] - 16).astype(f32))
            hits.append(jnp.where(column == ref[k, INDEX:EXPONENT, :], scale, 0.0).astype(bf16))
    both = dot(jnp.concatenate(hits, axis=1), codes)
    return both[:, :T] + both[:, T:]


def decode(blocks):
    return jnp.concatenate([decoded(ref[k, :HALF, :]) for ref in blocks for k in range(ref.shape[0])], axis=0)


def own_slots():
    lane_slot = lax.broadcasted_iota(jnp.int32, (GROUP, GROUP * T), 1) // T
    return lane_slot == lax.broadcasted_iota(jnp.int32, (GROUP, GROUP * T), 0)


def spread(rows, own):
    return jnp.where(own, jnp.concatenate([rows] * GROUP, axis=1).astype(f32), 0.0).astype(bf16)


def tile_terms(tiles, ready, picked, out):
    own = own_slots()
    for g in range(CHUNKS):
        ready(g)
        rows = slice(g * GROUP, (g + 1) * GROUP)
        out[rows, :] = dot(spread(picked[rows, :], own), tiles[rows].reshape(GROUP * T, T))


def turn_kernel(tiles, out):
    for s in range(S):
        out[s] = tiles[s].T


def first_route_kernel(
    count, flow_in, link_in, price_in, tiles, out, kept, index, sems, more, flow_row, link_row, price, picked, terms
):
    small = [
        pltpu.make_async_copy(a, b, more.at[i])
        for i, (a, b) in enumerate(((flow_in, flow_row), (link_in, link_row), (price_in, price)))
    ]

    def copy(g):
        rows = pl.ds(g * FETCH, FETCH)
        return pltpu.make_async_copy(tiles.at[rows], kept.at[rows], sems.at[g])

    for c in small:
        c.start()
    for g in range(S // FETCH):
        copy(g).start()
    for c in small:
        c.wait()
    used = count[0, 0]
    flow_used = used_index(flow_row[...], used)
    index[:S, :] = own_column(flow_row[...], used)
    column = own_column(link_row[...], used)
    index[S : 2 * S, :] = column
    index[2 * S : 2 * S + 1, :] = flow_used
    index[2 * S + 1 : 2 * S + 2, :] = used_index(link_row[...], used)
    at = lax.broadcasted_iota(jnp.int32, (S, T), 1)
    hits = [jnp.where(column == at + c * T, 1.0, 0.0).astype(bf16) for c in range(price.shape[0] // T)]
    picked[...] = dot(jnp.concatenate(hits, axis=1), price[...].astype(bf16)).astype(bf16)

    def ready(g):
        if g * GROUP % FETCH == 0:
            copy(g * GROUP // FETCH).wait()

    tile_terms(kept, ready, picked, terms)
    put_payload(out, terms[...], flow_used)


def load_kernel(index, own, tiles, *rest):
    blocks, (out, sent, terms) = rest[:-3], rest[-3:]
    route_sum = matched_sum(index[:S, :], blocks, decode(blocks))
    sent[...] = (own[0] / (own[1] + route_sum)).astype(bf16)
    tile_terms(tiles, lambda g: None, sent, terms)
    put_payload(out, terms[...], index[2 * S + 1 : 2 * S + 2, :])


def route_kernel(index, own, tiles, *rest):
    blocks, (out, picked, terms) = rest[:-3], rest[-3:]
    load = matched_sum(index[S : 2 * S, :], blocks, decode(blocks))
    picked[...] = (own[2] * jnp.exp(step_size * (load / own[3] - 1.0))).astype(bf16)
    tile_terms(tiles, lambda g: None, picked, terms)
    put_payload(out, terms[...], index[2 * S : 2 * S + 1, :])


def every_sum(blocks, code, hits, n, emit):
    code[...] = decode(blocks)
    rows = lax.broadcasted_iota(jnp.int32, (S, T), 0)
    chunk, scale = [], []
    for ref in blocks:
        for k in range(ref.shape[0]):
            index = ref[k, INDEX:EXPONENT, :]
            at = slice(len(chunk) * T, (len(chunk) + 1) * T)
            hits[:, at] = jnp.where(rows == (index & (T - 1)), 1.0, 0.0).astype(bf16)
            chunk.append(index >> 7)
            scale.append(jnp.exp2((ref[k, EXPONENT : EXPONENT + 1, :] - 16).astype(f32)))
    chunk = jnp.concatenate(chunk, axis=1)
    scale = jnp.concatenate(scale, axis=1)
    for c in range(n):
        mine = jnp.where(chunk == c, scale, 0.0)
        mine = jnp.broadcast_to(mine, (GROUP, mine.shape[1])).astype(bf16)
        both = dot(hits[...] * jnp.concatenate([mine] * (S // GROUP), axis=0), code[...])
        emit(slice(c * T, (c + 1) * T), both[:, :T] + both[:, T:])


def rate_kernel(weight, access, *rest):
    blocks, (out, code, hits, buf, sems) = rest[:-5], rest[-5:]
    copies = []

    def emit(rows, total):
        buf[rows, :] = weight[rows, :] / (access[rows, :] + total)
        copies.append(pltpu.make_async_copy(buf.at[rows], out.at[rows], sems.at[len(copies)]))
        copies[-1].start()

    every_sum(blocks, code, hits, out.shape[0] // T, emit)
    for c in copies:
        c.wait()


def first_price_kernel(price, capacity, *rest):
    blocks, (out, code, hits) = rest[:-3], rest[-3:]

    def emit(rows, total):
        out[rows, :] = price[rows, :] * jnp.exp(step_size * (total / capacity[rows, :] - 1.0))

    every_sum(blocks, code, hits, out.shape[0] // T, emit)


def last_price_kernel(price, capacity, *rest):
    blocks, (out, code, hits, buf, sems) = rest[:-5], rest[-5:]
    copies = []

    def emit(rows, total):
        buf[rows, :] = price[rows, :] * jnp.exp(step_size * (total / capacity[rows, :] - 1.0))
        copies.append(pltpu.make_async_copy(buf.at[rows], out.at[rows], sems.at[len(copies)]))
        copies[-1].start()

    every_sum(blocks, code, hits, out.shape[0] // T, emit)
    for c in copies:
        c.wait()


def prepare_kernel(
    flow_in, link_in, class_in, table_in, access_in, price_in, capacity_in,
    weight, own, access, price, capacity, sems, flow_at, link_at, flow_class, table,
):
    ends = (
        (class_in, flow_class),
        (table_in, table),
        (flow_in, flow_at),
        (link_in, link_at),
        (access_in, access),
        (price_in, price),
        (capacity_in, capacity),
    )
    copies = [pltpu.make_async_copy(a, b, sems.at[i]) for i, (a, b) in enumerate(ends)]
    for c in copies:
        c.start()
    for c in copies[:2]:
        c.wait()
    low = jnp.broadcast_to(table[0:1, :], (8, T))
    high = jnp.broadcast_to(table[1:2, :], (8, T))

    def look(r, carry):
        rows = pl.ds(pl.multiple_of(r * 8, 8), 8)
        which = flow_class[rows, :]
        lane = which & (T - 1)
        from_low = jnp.take_along_axis(low, lane, axis=1)
        from_high = jnp.take_along_axis(high, lane, axis=1)
        weight[rows, :] = jnp.where(which < T, from_low, from_high)
        return carry

    lax.fori_loop(0, flow_class.shape[0] // 8, look, 0, unroll=16)
    for c in copies[2:]:
        c.wait()

    def pick(s, carry):
        f = flow_at[0, s]
        l = link_at[0, s]
        own[0, pl.ds(s, 1), :] = weight[pl.ds(f, 1), :]
        own[1, pl.ds(s, 1), :] = access[pl.ds(f, 1), :]
        own[2, pl.ds(s, 1), :] = price[pl.ds(l, 1), :]
        own[3, pl.ds(s, 1), :] = capacity[pl.ds(l, 1), :]
        return carry

    lax.fori_loop(0, S, pick, 0, unroll=16)


def shifts():
    def device(y, core, x, z):
        return ((y % 4) * 2 + core) * 16 + (x % 4) * 4 + z % 4

    every = [(y, c, x, z) for y in range(4) for c in range(2) for x in range(4) for z in range(4)]

    def moved(f):
        return [(device(*p), device(*f(*p))) for p in every]

    order = (1, 3, 2)
    first = [moved(lambda y, c, x, z, d=d: (y, 1, x + d, z) if c == 0 else (y, 0, x, z + d)) for d in order]
    second = [moved(lambda y, c, x, z, d=d: (y, 1, x + d, z) if c == 0 else (y, 0, x, z + d)) for d in order]
    along_y = [moved(lambda y, c, x, z, d=d: (y + d, 1 - c, x, z)) for d in order]
    partner = moved(lambda y, c, x, z: (y, 1 - c, x, z))
    return first, second, along_y, partner


FIRST, SECOND, ALONG_Y, PARTNER = shifts()


def send(x, perm):
    return lax.ppermute(x, ("flow", "link"), perm)


def gather_link(x):
    near, far = [send(x, PARTNER)], []
    for p in FIRST:
        near.append(send(x, p))
    near = jnp.stack(near)
    for p in SECOND:
        far.append(send(near, p))
    return [send(near, PARTNER)] + far


def gather_flow(x):
    near = [x]
    for p in ALONG_Y:
        near.append(send(x, p))
    near = jnp.stack(near)
    return [near, send(near, PARTNER)]


def on_device(
    route_tiles,
    tile_count,
    tile_flow,
    tile_link,
    flow_class,
    class_weight,
    access_price,
    capacity,
    init_price,
):
    flow_blocks = access_price.shape[0] // T
    link_blocks = capacity.shape[0] // T
    cap = capacity.reshape(link_blocks, T)
    price = init_price.reshape(link_blocks, T)
    access = access_price.reshape(flow_blocks, T)
    payload = pltpu.VMEM((PAYLOAD, T), jnp.int32)

    def tile_call(body, own, tiles, blocks):
        return pl.pallas_call(
            body,
            out_shape=payload,
            in_specs=[VM] * (3 + len(blocks)),
            out_specs=VM,
            scratch_shapes=[pltpu.VMEM((S, T), bf16), pltpu.VMEM((S, T), f32)],
            compiler_params=PARAMS,
        )(in_vmem(index), in_vmem(own), in_vmem(tiles), *[in_vmem(x) for x in blocks])

    def full_call(body, a, b, blocks, last):
        pieces = sum(x.shape[0] for x in blocks)
        scratch = [pltpu.VMEM((pieces * S, 2 * T), bf16), pltpu.VMEM((S, pieces * S), bf16)]
        if last:
            scratch += [pltpu.VMEM(a.shape, f32), pltpu.SemaphoreType.DMA((a.shape[0] // T,))]
        return pl.pallas_call(
            body,
            out_shape=pltpu.HBM(a.shape, f32) if last else pltpu.VMEM(a.shape, f32),
            in_specs=[VM] * (2 + len(blocks)),
            out_specs=HB if last else VM,
            scratch_shapes=scratch,
            compiler_params=PARAMS,
        )(in_vmem(a), in_vmem(b), *[in_vmem(x) for x in blocks])

    route_one, tiles, index = pl.pallas_call(
        first_route_kernel,
        out_shape=(payload, pltpu.VMEM((S, T, T), bf16), pltpu.VMEM((2 * S + 8, T), jnp.int32)),
        in_specs=[SM] + [HB] * 4,
        out_specs=(VM, VM, VM),
        scratch_shapes=[
            pltpu.SemaphoreType.DMA((S // FETCH,)),
            pltpu.SemaphoreType.DMA((3,)),
            pltpu.VMEM((1, S), jnp.int32),
            pltpu.VMEM((1, S), jnp.int32),
            pltpu.VMEM(price.shape, f32),
            pltpu.VMEM((S, T), bf16),
            pltpu.VMEM((S, T), f32),
        ],
        compiler_params=PARAMS,
        name="first_route",
    )(tile_count, *[in_hbm(x) for x in (tile_flow, tile_link, price, route_tiles)])
    turned = pl.pallas_call(
        turn_kernel,
        out_shape=pltpu.VMEM((S, T, T), bf16),
        in_specs=[VM],
        out_specs=VM,
        compiler_params=PARAMS,
        name="turn",
    )(in_vmem(tiles))
    full = (access.shape, price.shape, cap.shape)
    weight, own, access, price, cap = pl.pallas_call(
        prepare_kernel,
        out_shape=(
            pltpu.VMEM((flow_blocks, T), f32),
            pltpu.VMEM((4, S, T), f32),
            *[pltpu.VMEM(shape, f32) for shape in full],
        ),
        in_specs=[HB] * 7,
        out_specs=(VM,) * 5,
        scratch_shapes=[
            pltpu.SemaphoreType.DMA((7,)),
            pltpu.SMEM((1, S), jnp.int32),
            pltpu.SMEM((1, S), jnp.int32),
            pltpu.VMEM((flow_blocks, T), jnp.int32),
            pltpu.VMEM((2, T), f32),
        ],
        compiler_params=PARAMS,
        name="prepare",
    )(
        *[
            in_hbm(x)
            for x in (
                tile_flow,
                tile_link,
                flow_class.reshape(flow_blocks, T),
                class_weight.reshape(2, T),
                access,
                price,
                cap,
            )
        ]
    )

    routes = gather_link(route_one)
    loads = gather_flow(tile_call(load_kernel, own, turned, routes))
    price_one = full_call(first_price_kernel, price, cap, loads, False)
    routes = gather_link(tile_call(route_kernel, own, tiles, loads))
    rate = full_call(rate_kernel, weight, access, routes, True)
    loads = gather_flow(tile_call(load_kernel, own, turned, routes))
    price_two = full_call(last_price_kernel, price_one, cap, loads, True)
    return (rate.reshape(-1), price_two.reshape(-1))


def solution(mesh):
    return jax.shard_map(
        on_device,
        mesh=mesh,
        in_specs=(
            P("flow", "link", None),
            P("flow", "link"),
            P("flow", "link"),
            P("flow", "link"),
            P("flow"),
            P(),
            P("flow"),
            P("link"),
            P("link"),
        ),
        out_specs=(P("flow"), P("link")),
        check_vma=False,
    )
```

```python
import jax
import jax.numpy as jnp
from jax import lax
from jax.experimental import pallas as pl
from jax.experimental.pallas import tpu as pltpu
from jax.sharding import PartitionSpec as P


step_size = 0.5


f32 = jnp.float32
bf16 = jnp.bfloat16

T = 128
S = 128
HALF = S // 2
PAYLOAD = HALF + 8
INDEX = HALF
EXPONENT = HALF + 1
GROUP = 16
CHUNKS = S // GROUP
FETCH = 64

SM = pl.BlockSpec(memory_space=pltpu.SMEM)
HB = pl.BlockSpec(memory_space=pltpu.HBM)
VM = pl.BlockSpec(memory_space=pltpu.VMEM)
PARAMS = pltpu.CompilerParams(vmem_limit_bytes=16 << 20)


def in_vmem(x):
    return pltpu.with_memory_space_constraint(x, pltpu.VMEM)


def in_hbm(x):
    return pltpu.with_memory_space_constraint(x, pltpu.HBM)


def dot(a, b):
    return lax.dot_general(a, b, (((1,), (0,)), ((), ())), preferred_element_type=f32)


def used_index(index_row, count, unused=-1):
    slot = lax.broadcasted_iota(jnp.int32, index_row.shape, 1)
    return jnp.where(slot < count, index_row, unused)


def own_column(index_row, count):
    row = used_index(index_row, count, -2).astype(f32)
    return jnp.broadcast_to(row, (S, S)).T.astype(jnp.int32)


def put_payload(out, terms, index_row):
    largest = jnp.max(terms, axis=1, keepdims=True)
    exponent = jnp.floor(jnp.log(jnp.maximum(largest, 1e-30)) * 1.4426950408889634) + 1.0
    scale = jnp.exp2(16.0 - exponent)
    coded = jnp.minimum(jnp.round(terms * scale), 65535.0).astype(jnp.int32)
    out[:HALF, :] = coded[:HALF, :] | (coded[HALF:, :] << 16)
    out[INDEX:EXPONENT, :] = index_row
    exponent_row = jnp.broadcast_to(exponent, (S, S)).T[:1, :].astype(jnp.int32)
    out[EXPONENT : EXPONENT + 1, :] = exponent_row


def decoded(words):
    top = lax.shift_right_logical(words, 16)
    high = jnp.concatenate([words & 0xFF00, top & 0xFF00], axis=0)
    low = jnp.concatenate([words & 0xFF, top & 0xFF], axis=0)
    return jnp.concatenate([high.astype(f32).astype(bf16), low.astype(f32).astype(bf16)], axis=1)


def matched_sum(column, blocks, codes):
    hits = []
    for ref in blocks:
        for k in range(ref.shape[0]):
            scale = jnp.exp2((ref[k, EXPONENT : EXPONENT + 1, :] - 16).astype(f32))
            hits.append(jnp.where(column == ref[k, INDEX:EXPONENT, :], scale, 0.0).astype(bf16))
    both = dot(jnp.concatenate(hits, axis=1), codes)
    return both[:, :T] + both[:, T:]


def decode(blocks):
    return jnp.concatenate([decoded(ref[k, :HALF, :]) for ref in blocks for k in range(ref.shape[0])], axis=0)


def own_slots():
    lane_slot = lax.broadcasted_iota(jnp.int32, (GROUP, GROUP * T), 1) // T
    return lane_slot == lax.broadcasted_iota(jnp.int32, (GROUP, GROUP * T), 0)


def spread(rows, own):
    return jnp.where(own, jnp.concatenate([rows] * GROUP, axis=1).astype(f32), 0.0).astype(bf16)


def tile_terms(tiles, ready, picked, out):
    own = own_slots()
    for g in range(CHUNKS):
        ready(g)
        rows = slice(g * GROUP, (g + 1) * GROUP)
        out[rows, :] = dot(spread(picked[rows, :], own), tiles[rows].reshape(GROUP * T, T))


def turn_kernel(tiles, *rest):
    sources, (out, *kept), sems = rest[:7], rest[7:15], rest[15]
    copies = [pltpu.make_async_copy(a, b, sems.at[i]) for i, (a, b) in enumerate(zip(sources, kept))]
    for c in copies:
        c.start()
    for s in range(S):
        out[s] = tiles[s].T
    for c in copies:
        c.wait()


def first_route_kernel(
    count, flow_in, link_in, price_in, tiles, out, kept, index, sems, more, flow_row, link_row, price, picked, terms
):
    small = [
        pltpu.make_async_copy(a, b, more.at[i])
        for i, (a, b) in enumerate(((flow_in, flow_row), (link_in, link_row), (price_in, price)))
    ]

    def copy(g):
        rows = pl.ds(g * FETCH, FETCH)
        return pltpu.make_async_copy(tiles.at[rows], kept.at[rows], sems.at[g])

    for c in small:
        c.start()
    for g in range(S // FETCH):
        copy(g).start(priority=min(g, 1))
    for c in small:
        c.wait()
    used = count[0, 0]
    flow_used = used_index(flow_row[...], used)
    index[:S, :] = own_column(flow_row[...], used)
    column = own_column(link_row[...], used)
    index[S : 2 * S, :] = column
    index[2 * S : 2 * S + 1, :] = flow_used
    index[2 * S + 1 : 2 * S + 2, :] = used_index(link_row[...], used)
    at = lax.broadcasted_iota(jnp.int32, (S, T), 1)
    hits = [jnp.where(column == at + c * T, 1.0, 0.0).astype(bf16) for c in range(price.shape[0] // T)]
    picked[...] = dot(jnp.concatenate(hits, axis=1), price[...].astype(bf16)).astype(bf16)

    def ready(g):
        if g * GROUP % FETCH == 0:
            copy(g * GROUP // FETCH).wait()

    tile_terms(kept, ready, picked, terms)
    put_payload(out, terms[...], flow_used)


def early_kernel(index, *rest):
    blocks, out = rest[:-1], rest[-1]
    out[...] = matched_sum(index[:S, :], blocks, decode(blocks))


def early_price_kernel(*rest):
    blocks, (out, code, hits) = rest[:-3], rest[-3:]

    def emit(rows, total):
        out[rows, :] = total

    every_sum(blocks, code, hits, out.shape[0] // T, emit)


def load_kernel(index, own, tiles, early, *rest):
    blocks, (out, sent, terms) = rest[:-3], rest[-3:]
    route_sum = early[...] + matched_sum(index[:S, :], blocks, decode(blocks))
    sent[...] = (own[0] / (own[1] + route_sum)).astype(bf16)
    tile_terms(tiles, lambda g: None, sent, terms)
    put_payload(out, terms[...], index[2 * S + 1 : 2 * S + 2, :])


def route_kernel(index, own, tiles, *rest):
    blocks, (out, picked, terms) = rest[:-3], rest[-3:]
    load = matched_sum(index[S : 2 * S, :], blocks, decode(blocks))
    picked[...] = (own[2] * jnp.exp(step_size * (load / own[3] - 1.0))).astype(bf16)
    tile_terms(tiles, lambda g: None, picked, terms)
    put_payload(out, terms[...], index[2 * S : 2 * S + 1, :])


def every_sum(blocks, code, hits, n, emit):
    code[...] = decode(blocks)
    rows = lax.broadcasted_iota(jnp.int32, (S, T), 0)
    chunk, scale = [], []
    for ref in blocks:
        for k in range(ref.shape[0]):
            index = ref[k, INDEX:EXPONENT, :]
            at = slice(len(chunk) * T, (len(chunk) + 1) * T)
            hits[:, at] = jnp.where(rows == (index & (T - 1)), 1.0, 0.0).astype(bf16)
            chunk.append(index >> 7)
            scale.append(jnp.exp2((ref[k, EXPONENT : EXPONENT + 1, :] - 16).astype(f32)))
    chunk = jnp.concatenate(chunk, axis=1)
    scale = jnp.concatenate(scale, axis=1)
    for c in range(n):
        mine = jnp.where(chunk == c, scale, 0.0)
        mine = jnp.broadcast_to(mine, (GROUP, mine.shape[1])).astype(bf16)
        both = dot(hits[...] * jnp.concatenate([mine] * (S // GROUP), axis=0), code[...])
        emit(slice(c * T, (c + 1) * T), both[:, :T] + both[:, T:])


def rate_kernel(weight, access, *rest):
    blocks, (out, code, hits) = rest[:-3], rest[-3:]

    def emit(rows, total):
        out[rows, :] = weight[rows, :] / (access[rows, :] + total)

    every_sum(blocks, code, hits, out.shape[0] // T, emit)


def first_price_kernel(price, capacity, *rest):
    blocks, (out, code, hits) = rest[:-3], rest[-3:]

    def emit(rows, total):
        out[rows, :] = price[rows, :] * jnp.exp(step_size * (total / capacity[rows, :] - 1.0))

    every_sum(blocks, code, hits, out.shape[0] // T, emit)


def last_price_kernel(price, capacity, early, rate, *rest):
    blocks, (out, rate_out, code, hits, buf, sems) = rest[:-6], rest[-6:]
    copies = [pltpu.make_async_copy(rate, rate_out, sems.at[0])]
    copies[0].start()

    def emit(rows, total):
        buf[rows, :] = price[rows, :] * jnp.exp(step_size * ((early[rows, :] + total) / capacity[rows, :] - 1.0))
        copies.append(pltpu.make_async_copy(buf.at[rows], out.at[rows], sems.at[len(copies)]))
        copies[-1].start()

    every_sum(blocks, code, hits, out.shape[0] // T, emit)
    for c in copies:
        c.wait()


def prepare_kernel(flow_at, link_at, flow_class, table, access, price, capacity, weight, own):
    low = jnp.broadcast_to(table[0:1, :], (8, T))
    high = jnp.broadcast_to(table[1:2, :], (8, T))

    def look(r, carry):
        rows = pl.ds(pl.multiple_of(r * 8, 8), 8)
        which = flow_class[rows, :]
        lane = which & (T - 1)
        from_low = jnp.take_along_axis(low, lane, axis=1)
        from_high = jnp.take_along_axis(high, lane, axis=1)
        weight[rows, :] = jnp.where(which < T, from_low, from_high)
        return carry

    lax.fori_loop(0, flow_class.shape[0] // 8, look, 0, unroll=16)

    def pick(s, carry):
        f = flow_at[0, s]
        l = link_at[0, s]
        own[0, pl.ds(s, 1), :] = weight[pl.ds(f, 1), :]
        own[1, pl.ds(s, 1), :] = access[pl.ds(f, 1), :]
        own[2, pl.ds(s, 1), :] = price[pl.ds(l, 1), :]
        own[3, pl.ds(s, 1), :] = capacity[pl.ds(l, 1), :]
        return carry

    lax.fori_loop(0, S, pick, 0, unroll=16)


def shifts():
    def device(y, core, x, z):
        return ((y % 4) * 2 + core) * 16 + (x % 4) * 4 + z % 4

    every = [(y, c, x, z) for y in range(4) for c in range(2) for x in range(4) for z in range(4)]

    def moved(f):
        return [(device(*p), device(*f(*p))) for p in every]

    order = (1, 3, 2)
    first = [moved(lambda y, c, x, z, d=d: (y, 1, x + d, z) if c == 0 else (y, 0, x, z + d)) for d in order]
    second = [moved(lambda y, c, x, z, d=d: (y, 1, x + d, z) if c == 0 else (y, 0, x, z + d)) for d in order]
    along_y = [moved(lambda y, c, x, z, d=d: (y + d, 1 - c, x, z)) for d in order]
    partner = moved(lambda y, c, x, z: (y, 1 - c, x, z))
    return first, second, along_y, partner


FIRST, SECOND, ALONG_Y, PARTNER = shifts()


def send(x, perm):
    return lax.ppermute(x, ("flow", "link"), perm)


def gather_link(x):
    near, far = [send(x, PARTNER)], []
    for p in FIRST:
        near.append(send(x, p))
    near = jnp.stack(near)
    for p in SECOND:
        far.append(send(near, p))
    return [send(near, PARTNER)] + far


def gather_flow(x):
    near = [x]
    for p in ALONG_Y:
        near.append(send(x, p))
    near = jnp.stack(near)
    return [near, send(near, PARTNER)]


def on_device(
    route_tiles,
    tile_count,
    tile_flow,
    tile_link,
    flow_class,
    class_weight,
    access_price,
    capacity,
    init_price,
):
    flow_blocks = access_price.shape[0] // T
    link_blocks = capacity.shape[0] // T
    cap = capacity.reshape(link_blocks, T)
    price = init_price.reshape(link_blocks, T)
    access = access_price.reshape(flow_blocks, T)
    payload = pltpu.VMEM((PAYLOAD, T), jnp.int32)

    def early_call(blocks):
        return pl.pallas_call(
            early_kernel,
            out_shape=pltpu.VMEM((S, T), f32),
            in_specs=[VM] * (1 + len(blocks)),
            out_specs=VM,
            compiler_params=PARAMS,
        )(in_vmem(index), *[in_vmem(x) for x in blocks])

    def load_call(routes):
        early = early_call([routes[0]] + routes[2:])
        return tile_call(load_kernel, own, turned, [early], [routes[1]])

    def tile_call(body, own, tiles, early, blocks):
        return pl.pallas_call(
            body,
            out_shape=payload,
            in_specs=[VM] * (3 + len(early) + len(blocks)),
            out_specs=VM,
            scratch_shapes=[pltpu.VMEM((S, T), bf16), pltpu.VMEM((S, T), f32)],
            compiler_params=PARAMS,
        )(in_vmem(index), in_vmem(own), in_vmem(tiles), *[in_vmem(x) for x in early + blocks])

    def early_price_call(blocks):
        pieces = sum(x.shape[0] for x in blocks)
        return pl.pallas_call(
            early_price_kernel,
            out_shape=pltpu.VMEM(price.shape, f32),
            in_specs=[VM] * len(blocks),
            out_specs=VM,
            scratch_shapes=[pltpu.VMEM((pieces * S, 2 * T), bf16), pltpu.VMEM((S, pieces * S), bf16)],
            compiler_params=PARAMS,
        )(*[in_vmem(x) for x in blocks])

    def full_call(body, a, b, early, blocks, last):
        pieces = sum(x.shape[0] for x in blocks)
        scratch = [pltpu.VMEM((pieces * S, 2 * T), bf16), pltpu.VMEM((S, pieces * S), bf16)]
        if last:
            scratch += [pltpu.VMEM(a.shape, f32), pltpu.SemaphoreType.DMA((1 + a.shape[0] // T,))]
        return pl.pallas_call(
            body,
            out_shape=tuple(pltpu.HBM(x.shape, f32) for x in (a, early[1])) if last else pltpu.VMEM(a.shape, f32),
            in_specs=[VM] * (2 + len(early) + len(blocks)),
            out_specs=(HB, HB) if last else VM,
            scratch_shapes=scratch,
            compiler_params=PARAMS,
        )(in_vmem(a), in_vmem(b), *[in_vmem(x) for x in early + blocks])

    route_one, tiles, index = pl.pallas_call(
        first_route_kernel,
        out_shape=(payload, pltpu.VMEM((S, T, T), bf16), pltpu.VMEM((2 * S + 8, T), jnp.int32)),
        in_specs=[SM] + [HB] * 4,
        out_specs=(VM, VM, VM),
        scratch_shapes=[
            pltpu.SemaphoreType.DMA((S // FETCH,)),
            pltpu.SemaphoreType.DMA((3,)),
            pltpu.VMEM((1, S), jnp.int32),
            pltpu.VMEM((1, S), jnp.int32),
            pltpu.VMEM(price.shape, f32),
            pltpu.VMEM((S, T), bf16),
            pltpu.VMEM((S, T), f32),
        ],
        compiler_params=PARAMS,
        name="first_route",
    )(tile_count, *[in_hbm(x) for x in (tile_flow, tile_link, price, route_tiles)])
    fetched = (
        pltpu.SMEM((1, S), jnp.int32),
        pltpu.SMEM((1, S), jnp.int32),
        pltpu.VMEM((flow_blocks, T), jnp.int32),
        pltpu.VMEM((2, T), f32),
        pltpu.VMEM(access.shape, f32),
        pltpu.VMEM(price.shape, f32),
        pltpu.VMEM(cap.shape, f32),
    )
    sources = (tile_flow, tile_link, flow_class.reshape(flow_blocks, T), class_weight.reshape(2, T), access, price, cap)
    turned, flow_at, link_at, *sources = pl.pallas_call(
        turn_kernel,
        out_shape=(pltpu.VMEM((S, T, T), bf16), *fetched),
        in_specs=[VM] + [HB] * 7,
        out_specs=(VM, SM, SM) + (VM,) * 5,
        scratch_shapes=[pltpu.SemaphoreType.DMA((7,))],
        compiler_params=PARAMS,
        name="turn",
    )(in_vmem(tiles), *[in_hbm(x) for x in sources])
    access, price, cap = sources[2:]
    weight, own = pl.pallas_call(
        prepare_kernel,
        out_shape=(pltpu.VMEM((flow_blocks, T), f32), pltpu.VMEM((4, S, T), f32)),
        in_specs=[SM, SM] + [VM] * 5,
        out_specs=(VM, VM),
        compiler_params=PARAMS,
        name="prepare",
    )(flow_at, link_at, *[in_vmem(x) for x in sources])

    routes = gather_link(route_one)
    loads = gather_flow(load_call(routes))
    price_one = full_call(first_price_kernel, price, cap, [], loads, False)
    routes = gather_link(tile_call(route_kernel, own, tiles, [], loads))
    rate = full_call(rate_kernel, weight, access, [], routes, False)
    loads = gather_flow(load_call(routes))
    early = early_price_call(loads[:1])
    price_two, rate = full_call(last_price_kernel, price_one, cap, [early, rate], loads[1:], True)
    return (rate.reshape(-1), price_two.reshape(-1))


def solution(mesh):
    return jax.shard_map(
        on_device,
        mesh=mesh,
        in_specs=(
            P("flow", "link", None),
            P("flow", "link"),
            P("flow", "link"),
            P("flow", "link"),
            P("flow"),
            P(),
            P("flow"),
            P("link"),
            P("link"),
        ),
        out_specs=(P("flow"), P("link")),
        check_vma=False,
    )
```

```python
import jax
import jax.numpy as jnp
from jax import lax
from jax.experimental import pallas as pl
from jax.experimental.pallas import tpu as pltpu
from jax.sharding import PartitionSpec as P


step_size = 0.5


f32 = jnp.float32
bf16 = jnp.bfloat16

T = 128
S = 128
HALF = S // 2
PAYLOAD = HALF + 8
INDEX = HALF
EXPONENT = HALF + 1
PIECES = 4
GROUP = 16
CHUNKS = S // GROUP
FETCH = 64

SM = pl.BlockSpec(memory_space=pltpu.SMEM)
HB = pl.BlockSpec(memory_space=pltpu.HBM)
VM = pl.BlockSpec(memory_space=pltpu.VMEM)
PARAMS = pltpu.CompilerParams(vmem_limit_bytes=16 << 20)


def in_vmem(x):
    return pltpu.with_memory_space_constraint(x, pltpu.VMEM)


def in_hbm(x):
    return pltpu.with_memory_space_constraint(x, pltpu.HBM)


def dot(a, b):
    return lax.dot_general(a, b, (((1,), (0,)), ((), ())), preferred_element_type=f32)


def used_index(index_row, count, unused=-1):
    slot = lax.broadcasted_iota(jnp.int32, index_row.shape, 1)
    return jnp.where(slot < count, index_row, unused)


def own_column(index_row, count):
    row = used_index(index_row, count, -2).astype(f32)
    return jnp.broadcast_to(row, (S, S)).T.astype(jnp.int32)


def put_payload(out, terms, index_row):
    largest = jnp.max(terms, axis=1, keepdims=True)
    exponent = jnp.floor(jnp.log(jnp.maximum(largest, 1e-30)) * 1.4426950408889634) + 1.0
    scale = jnp.exp2(16.0 - exponent)
    coded = jnp.minimum(jnp.round(terms * scale), 65535.0).astype(jnp.int32)
    out[:HALF, :] = coded[:HALF, :] | (coded[HALF:, :] << 16)
    out[INDEX:EXPONENT, :] = index_row
    exponent_row = jnp.broadcast_to(exponent, (S, S)).T[:1, :].astype(jnp.int32)
    out[EXPONENT : EXPONENT + 1, :] = exponent_row


def decoded(words):
    top = lax.shift_right_logical(words, 16)
    high = jnp.concatenate([words & 0xFF00, top & 0xFF00], axis=0)
    low = jnp.concatenate([words & 0xFF, top & 0xFF], axis=0)
    return jnp.concatenate([high.astype(f32).astype(bf16), low.astype(f32).astype(bf16)], axis=1)


def matched_sum(column, blocks, codes):
    hits = []
    for ref in blocks:
        for k in range(PIECES):
            index, scale = index_and_scale(ref, k)
            hits.append(jnp.where(column == index, scale, 0.0).astype(bf16))
    both = dot(jnp.concatenate(hits, axis=1), codes)
    return both[:, :T] + both[:, T:]


def decode(blocks):
    words = [ref[k * HALF : (k + 1) * HALF, :] for ref in blocks for k in range(PIECES)]
    return jnp.concatenate([decoded(w) for w in words], axis=0)


def index_and_scale(ref, k):
    at = PIECES * HALF + 2 * k
    return ref[at : at + 1, :], jnp.exp2((ref[at + 1 : at + 2, :] - 16).astype(f32))


def join_kernel(*refs):
    payloads, out = refs[:-1], refs[-1]
    for k, p in enumerate(payloads):
        out[k * HALF : (k + 1) * HALF, :] = p[:HALF, :]
        at = PIECES * HALF + 2 * k
        out[at : at + 2, :] = p[INDEX : EXPONENT + 1, :]


def gathered(payloads):
    return pl.pallas_call(
        join_kernel,
        out_shape=pltpu.VMEM((PIECES * HALF + 2 * PIECES, T), jnp.int32),
        in_specs=[VM] * PIECES,
        out_specs=VM,
        compiler_params=PARAMS,
        name="join",
    )(*[in_vmem(p) for p in payloads])


def own_slots():
    lane_slot = lax.broadcasted_iota(jnp.int32, (GROUP, GROUP * T), 1) // T
    return lane_slot == lax.broadcasted_iota(jnp.int32, (GROUP, GROUP * T), 0)


def spread(rows, own):
    return jnp.where(own, jnp.concatenate([rows] * GROUP, axis=1).astype(f32), 0.0).astype(bf16)


def tile_terms(tiles, ready, picked, out):
    own = own_slots()
    for g in range(CHUNKS):
        ready(g)
        rows = slice(g * GROUP, (g + 1) * GROUP)
        out[rows, :] = dot(spread(picked[rows, :], own), tiles[rows].reshape(GROUP * T, T))


def turn_kernel(tiles, *rest):
    sources, (out, *kept), sems = rest[:7], rest[7:15], rest[15]
    copies = [pltpu.make_async_copy(a, b, sems.at[i]) for i, (a, b) in enumerate(zip(sources, kept))]
    for c in copies:
        c.start()
    for s in range(S):
        out[s] = tiles[s].T
    for c in copies:
        c.wait()


def first_route_kernel(
    count, flow_in, link_in, price_in, tiles, out, kept, index, sems, more, flow_row, link_row, price, picked, terms
):
    small = [
        pltpu.make_async_copy(a, b, more.at[i])
        for i, (a, b) in enumerate(((flow_in, flow_row), (link_in, link_row), (price_in, price)))
    ]

    def copy(g):
        rows = pl.ds(g * FETCH, FETCH)
        return pltpu.make_async_copy(tiles.at[rows], kept.at[rows], sems.at[g])

    for c in small:
        c.start()
    for g in range(S // FETCH):
        copy(g).start(priority=min(g, 1))
    for c in small:
        c.wait()
    used = count[0, 0]
    flow_used = used_index(flow_row[...], used)
    index[:S, :] = own_column(flow_row[...], used)
    column = own_column(link_row[...], used)
    index[S : 2 * S, :] = column
    index[2 * S : 2 * S + 1, :] = flow_used
    index[2 * S + 1 : 2 * S + 2, :] = used_index(link_row[...], used)
    at = lax.broadcasted_iota(jnp.int32, (S, T), 1)
    hits = [jnp.where(column == at + c * T, 1.0, 0.0).astype(bf16) for c in range(price.shape[0] // T)]
    picked[...] = dot(jnp.concatenate(hits, axis=1), price[...].astype(bf16)).astype(bf16)

    def ready(g):
        if g * GROUP % FETCH == 0:
            copy(g * GROUP // FETCH).wait()

    tile_terms(kept, ready, picked, terms)
    put_payload(out, terms[...], flow_used)


def early_kernel(index, *rest):
    blocks, out = rest[:-1], rest[-1]
    out[...] = matched_sum(index[:S, :], blocks, decode(blocks))


def early_price_kernel(*rest):
    blocks, (out, code, hits) = rest[:-3], rest[-3:]

    def emit(rows, total):
        out[rows, :] = total

    every_sum(blocks, code, hits, out.shape[0] // T, emit)


def load_kernel(index, own, tiles, early, *rest):
    blocks, (out, sent, terms) = rest[:-3], rest[-3:]
    route_sum = early[...] + matched_sum(index[:S, :], blocks, decode(blocks))
    sent[...] = (own[0] / (own[1] + route_sum)).astype(bf16)
    tile_terms(tiles, lambda g: None, sent, terms)
    put_payload(out, terms[...], index[2 * S + 1 : 2 * S + 2, :])


def route_kernel(index, own, tiles, *rest):
    blocks, (out, picked, terms) = rest[:-3], rest[-3:]
    load = matched_sum(index[S : 2 * S, :], blocks, decode(blocks))
    picked[...] = (own[2] * jnp.exp(step_size * (load / own[3] - 1.0))).astype(bf16)
    tile_terms(tiles, lambda g: None, picked, terms)
    put_payload(out, terms[...], index[2 * S : 2 * S + 1, :])


def every_sum(blocks, code, hits, n, emit):
    code[...] = decode(blocks)
    rows = lax.broadcasted_iota(jnp.int32, (S, T), 0)
    chunk, scale = [], []
    for ref in blocks:
        for k in range(PIECES):
            index, factor = index_and_scale(ref, k)
            at = slice(len(chunk) * T, (len(chunk) + 1) * T)
            hits[:, at] = jnp.where(rows == (index & (T - 1)), 1.0, 0.0).astype(bf16)
            chunk.append(index >> 7)
            scale.append(factor)
    chunk = jnp.concatenate(chunk, axis=1)
    scale = jnp.concatenate(scale, axis=1)
    for c in range(n):
        mine = jnp.where(chunk == c, scale, 0.0)
        mine = jnp.broadcast_to(mine, (GROUP, mine.shape[1])).astype(bf16)
        both = dot(hits[...] * jnp.concatenate([mine] * (S // GROUP), axis=0), code[...])
        emit(slice(c * T, (c + 1) * T), both[:, :T] + both[:, T:])


def rate_kernel(weight, access, *rest):
    blocks, (out, code, hits) = rest[:-3], rest[-3:]

    def emit(rows, total):
        out[rows, :] = weight[rows, :] / (access[rows, :] + total)

    every_sum(blocks, code, hits, out.shape[0] // T, emit)


def first_price_kernel(price, capacity, *rest):
    blocks, (out, code, hits) = rest[:-3], rest[-3:]

    def emit(rows, total):
        out[rows, :] = price[rows, :] * jnp.exp(step_size * (total / capacity[rows, :] - 1.0))

    every_sum(blocks, code, hits, out.shape[0] // T, emit)


def last_price_kernel(price, capacity, early, rate, *rest):
    blocks, (out, rate_out, code, hits, buf, sems) = rest[:-6], rest[-6:]
    copies = [pltpu.make_async_copy(rate, rate_out, sems.at[0])]
    copies[0].start()

    def emit(rows, total):
        buf[rows, :] = price[rows, :] * jnp.exp(step_size * ((early[rows, :] + total) / capacity[rows, :] - 1.0))
        copies.append(pltpu.make_async_copy(buf.at[rows], out.at[rows], sems.at[len(copies)]))
        copies[-1].start()

    every_sum(blocks, code, hits, out.shape[0] // T, emit)
    for c in copies:
        c.wait()


def prepare_kernel(flow_at, link_at, flow_class, table, access, price, capacity, weight, own):
    low = jnp.broadcast_to(table[0:1, :], (8, T))
    high = jnp.broadcast_to(table[1:2, :], (8, T))

    def look(r, carry):
        rows = pl.ds(pl.multiple_of(r * 8, 8), 8)
        which = flow_class[rows, :]
        lane = which & (T - 1)
        from_low = jnp.take_along_axis(low, lane, axis=1)
        from_high = jnp.take_along_axis(high, lane, axis=1)
        weight[rows, :] = jnp.where(which < T, from_low, from_high)
        return carry

    lax.fori_loop(0, flow_class.shape[0] // 8, look, 0, unroll=16)

    def pick(s, carry):
        f = flow_at[0, s]
        l = link_at[0, s]
        own[0, pl.ds(s, 1), :] = weight[pl.ds(f, 1), :]
        own[1, pl.ds(s, 1), :] = access[pl.ds(f, 1), :]
        own[2, pl.ds(s, 1), :] = price[pl.ds(l, 1), :]
        own[3, pl.ds(s, 1), :] = capacity[pl.ds(l, 1), :]
        return carry

    lax.fori_loop(0, S, pick, 0, unroll=16)


def shifts():
    def device(y, core, x, z):
        return ((y % 4) * 2 + core) * 16 + (x % 4) * 4 + z % 4

    every = [(y, c, x, z) for y in range(4) for c in range(2) for x in range(4) for z in range(4)]

    def moved(f):
        return [(device(*p), device(*f(*p))) for p in every]

    order = (1, 3, 2)
    first = [moved(lambda y, c, x, z, d=d: (y, 1, x + d, z) if c == 0 else (y, 0, x, z + d)) for d in order]
    second = [moved(lambda y, c, x, z, d=d: (y, 1, x + d, z) if c == 0 else (y, 0, x, z + d)) for d in order]
    along_y = [moved(lambda y, c, x, z, d=d: (y + d, 1 - c, x, z)) for d in order]
    partner = moved(lambda y, c, x, z: (y, 1 - c, x, z))
    return first, second, along_y, partner


FIRST, SECOND, ALONG_Y, PARTNER = shifts()


def send(x, perm):
    return lax.ppermute(x, ("flow", "link"), perm)


def gather_link(x):
    near, far = [send(x, PARTNER)], []
    for p in FIRST:
        near.append(send(x, p))
    near = gathered(near)
    for p in SECOND:
        far.append(send(near, p))
    return [send(near, PARTNER)] + far


def gather_flow(x):
    near = [x]
    for p in ALONG_Y:
        near.append(send(x, p))
    near = gathered(near)
    return [near, send(near, PARTNER)]


def on_device(
    route_tiles,
    tile_count,
    tile_flow,
    tile_link,
    flow_class,
    class_weight,
    access_price,
    capacity,
    init_price,
):
    flow_blocks = access_price.shape[0] // T
    link_blocks = capacity.shape[0] // T
    cap = capacity.reshape(link_blocks, T)
    price = init_price.reshape(link_blocks, T)
    access = access_price.reshape(flow_blocks, T)
    payload = pltpu.VMEM((PAYLOAD, T), jnp.int32)

    def early_call(blocks):
        return pl.pallas_call(
            early_kernel,
            out_shape=pltpu.VMEM((S, T), f32),
            in_specs=[VM] * (1 + len(blocks)),
            out_specs=VM,
            compiler_params=PARAMS,
        )(in_vmem(index), *[in_vmem(x) for x in blocks])

    def load_call(routes):
        early = early_call([routes[0]] + routes[2:])
        return tile_call(load_kernel, own, turned, [early], [routes[1]])

    def tile_call(body, own, tiles, early, blocks):
        return pl.pallas_call(
            body,
            out_shape=payload,
            in_specs=[VM] * (3 + len(early) + len(blocks)),
            out_specs=VM,
            scratch_shapes=[pltpu.VMEM((S, T), bf16), pltpu.VMEM((S, T), f32)],
            compiler_params=PARAMS,
        )(in_vmem(index), in_vmem(own), in_vmem(tiles), *[in_vmem(x) for x in early + blocks])

    def early_price_call(blocks):
        pieces = PIECES * len(blocks)
        return pl.pallas_call(
            early_price_kernel,
            out_shape=pltpu.VMEM(price.shape, f32),
            in_specs=[VM] * len(blocks),
            out_specs=VM,
            scratch_shapes=[pltpu.VMEM((pieces * S, 2 * T), bf16), pltpu.VMEM((S, pieces * S), bf16)],
            compiler_params=PARAMS,
        )(*[in_vmem(x) for x in blocks])

    def full_call(body, a, b, early, blocks, last):
        pieces = PIECES * len(blocks)
        scratch = [pltpu.VMEM((pieces * S, 2 * T), bf16), pltpu.VMEM((S, pieces * S), bf16)]
        if last:
            scratch += [pltpu.VMEM(a.shape, f32), pltpu.SemaphoreType.DMA((1 + a.shape[0] // T,))]
        return pl.pallas_call(
            body,
            out_shape=tuple(pltpu.HBM(x.shape, f32) for x in (a, early[1])) if last else pltpu.VMEM(a.shape, f32),
            in_specs=[VM] * (2 + len(early) + len(blocks)),
            out_specs=(HB, HB) if last else VM,
            scratch_shapes=scratch,
            compiler_params=PARAMS,
        )(in_vmem(a), in_vmem(b), *[in_vmem(x) for x in early + blocks])

    route_one, tiles, index = pl.pallas_call(
        first_route_kernel,
        out_shape=(payload, pltpu.VMEM((S, T, T), bf16), pltpu.VMEM((2 * S + 8, T), jnp.int32)),
        in_specs=[SM] + [HB] * 4,
        out_specs=(VM, VM, VM),
        scratch_shapes=[
            pltpu.SemaphoreType.DMA((S // FETCH,)),
            pltpu.SemaphoreType.DMA((3,)),
            pltpu.VMEM((1, S), jnp.int32),
            pltpu.VMEM((1, S), jnp.int32),
            pltpu.VMEM(price.shape, f32),
            pltpu.VMEM((S, T), bf16),
            pltpu.VMEM((S, T), f32),
        ],
        compiler_params=PARAMS,
        name="first_route",
    )(tile_count, *[in_hbm(x) for x in (tile_flow, tile_link, price, route_tiles)])
    fetched = (
        pltpu.SMEM((1, S), jnp.int32),
        pltpu.SMEM((1, S), jnp.int32),
        pltpu.VMEM((flow_blocks, T), jnp.int32),
        pltpu.VMEM((2, T), f32),
        pltpu.VMEM(access.shape, f32),
        pltpu.VMEM(price.shape, f32),
        pltpu.VMEM(cap.shape, f32),
    )
    sources = (tile_flow, tile_link, flow_class.reshape(flow_blocks, T), class_weight.reshape(2, T), access, price, cap)
    turned, flow_at, link_at, *sources = pl.pallas_call(
        turn_kernel,
        out_shape=(pltpu.VMEM((S, T, T), bf16), *fetched),
        in_specs=[VM] + [HB] * 7,
        out_specs=(VM, SM, SM) + (VM,) * 5,
        scratch_shapes=[pltpu.SemaphoreType.DMA((7,))],
        compiler_params=PARAMS,
        name="turn",
    )(in_vmem(tiles), *[in_hbm(x) for x in sources])
    access, price, cap = sources[2:]
    weight, own = pl.pallas_call(
        prepare_kernel,
        out_shape=(pltpu.VMEM((flow_blocks, T), f32), pltpu.VMEM((4, S, T), f32)),
        in_specs=[SM, SM] + [VM] * 5,
        out_specs=(VM, VM),
        compiler_params=PARAMS,
        name="prepare",
    )(flow_at, link_at, *[in_vmem(x) for x in sources])

    routes = gather_link(route_one)
    loads = gather_flow(load_call(routes))
    price_one = full_call(first_price_kernel, price, cap, [], loads, False)
    routes = gather_link(tile_call(route_kernel, own, tiles, [], loads))
    rate = full_call(rate_kernel, weight, access, [], routes, False)
    loads = gather_flow(load_call(routes))
    early = early_price_call(loads[:1])
    price_two, rate = full_call(last_price_kernel, price_one, cap, [early, rate], loads[1:], True)
    return (rate.reshape(-1), price_two.reshape(-1))


def solution(mesh):
    return jax.shard_map(
        on_device,
        mesh=mesh,
        in_specs=(
            P("flow", "link", None),
            P("flow", "link"),
            P("flow", "link"),
            P("flow", "link"),
            P("flow"),
            P(),
            P("flow"),
            P("link"),
            P("link"),
        ),
        out_specs=(P("flow"), P("link")),
        check_vma=False,
    )
```

```python
import jax
import jax.numpy as jnp
from jax import lax
from jax.experimental import pallas as pl
from jax.experimental.pallas import tpu as pltpu
from jax.sharding import PartitionSpec as P


step_size = 0.5


f32 = jnp.float32
bf16 = jnp.bfloat16

T = 128
S = 128
HALF = S // 2
PAYLOAD = HALF + 8
INDEX = HALF
EXPONENT = HALF + 1
PIECES = 4
GROUP = 16
CHUNKS = S // GROUP
FETCH = 64

SM = pl.BlockSpec(memory_space=pltpu.SMEM)
HB = pl.BlockSpec(memory_space=pltpu.HBM)
VM = pl.BlockSpec(memory_space=pltpu.VMEM)
PARAMS = pltpu.CompilerParams(vmem_limit_bytes=16 << 20)


def in_vmem(x):
    return pltpu.with_memory_space_constraint(x, pltpu.VMEM)


def in_hbm(x):
    return pltpu.with_memory_space_constraint(x, pltpu.HBM)


def dot(a, b):
    return lax.dot_general(a, b, (((1,), (0,)), ((), ())), preferred_element_type=f32)


def used_index(index_row, count, unused=-1):
    slot = lax.broadcasted_iota(jnp.int32, index_row.shape, 1)
    return jnp.where(slot < count, index_row, unused)


def own_column(index_row, count):
    row = used_index(index_row, count, -2).astype(f32)
    return jnp.broadcast_to(row, (S, S)).T.astype(jnp.int32)


def put_payload(out, terms, index_row):
    largest = jnp.max(terms, axis=1, keepdims=True)
    exponent = jnp.floor(jnp.log(jnp.maximum(largest, 1e-30)) * 1.4426950408889634) + 1.0
    scale = jnp.exp2(16.0 - exponent)
    coded = jnp.minimum(jnp.round(terms * scale), 65535.0).astype(jnp.int32)
    out[:HALF, :] = coded[:HALF, :] | (coded[HALF:, :] << 16)
    out[INDEX:EXPONENT, :] = index_row
    exponent_row = jnp.broadcast_to(exponent, (S, S)).T[:1, :].astype(jnp.int32)
    out[EXPONENT : EXPONENT + 1, :] = exponent_row


def decoded(words):
    top = lax.shift_right_logical(words, 16)
    high = jnp.concatenate([words & 0xFF00, top & 0xFF00], axis=0)
    low = jnp.concatenate([words & 0xFF, top & 0xFF], axis=0)
    return jnp.concatenate([high.astype(f32).astype(bf16), low.astype(f32).astype(bf16)], axis=1)


def matched_sum(column, blocks, codes):
    hits = []
    for ref in blocks:
        for k in range(PIECES):
            index, scale = index_and_scale(ref, k)
            hits.append(jnp.where(column == index, scale, 0.0).astype(bf16))
    both = dot(jnp.concatenate(hits, axis=1), codes)
    return both[:, :T] + both[:, T:]


def decode(blocks):
    words = [ref[k * HALF : (k + 1) * HALF, :] for ref in blocks for k in range(PIECES)]
    return jnp.concatenate([decoded(w) for w in words], axis=0)


def index_and_scale(ref, k):
    at = PIECES * HALF + 2 * k
    return ref[at : at + 1, :], jnp.exp2((ref[at + 1 : at + 2, :] - 16).astype(f32))


def join_kernel(*refs):
    payloads, out = refs[:-1], refs[-1]
    for k, p in enumerate(payloads):
        out[k * HALF : (k + 1) * HALF, :] = p[:HALF, :]
        at = PIECES * HALF + 2 * k
        out[at : at + 2, :] = p[INDEX : EXPONENT + 1, :]


def gathered(payloads):
    return pl.pallas_call(
        join_kernel,
        out_shape=pltpu.VMEM((PIECES * HALF + 2 * PIECES, T), jnp.int32),
        in_specs=[VM] * PIECES,
        out_specs=VM,
        compiler_params=PARAMS,
        name="join",
    )(*[in_vmem(p) for p in payloads])


def own_slots():
    lane_slot = lax.broadcasted_iota(jnp.int32, (GROUP, GROUP * T), 1) // T
    return lane_slot == lax.broadcasted_iota(jnp.int32, (GROUP, GROUP * T), 0)


def spread(rows, own):
    return jnp.where(own, jnp.concatenate([rows] * GROUP, axis=1).astype(f32), 0.0).astype(bf16)


def tile_terms(tiles, ready, picked, out):
    own = own_slots()
    for g in range(CHUNKS):
        ready(g)
        rows = slice(g * GROUP, (g + 1) * GROUP)
        out[rows, :] = dot(spread(picked[rows, :], own), tiles[rows].reshape(GROUP * T, T))


def turn_kernel(tiles, *rest):
    sources, (out, *kept), sems = rest[:7], rest[7:15], rest[15]
    copies = [pltpu.make_async_copy(a, b, sems.at[i]) for i, (a, b) in enumerate(zip(sources, kept))]
    for c in copies:
        c.start()
    for s in range(S):
        out[s] = tiles[s].T
    for c in copies:
        c.wait()


def first_route_kernel(
    count, flow_in, link_in, price_in, tiles, out, kept, index, sems, more, flow_row, link_row, price, picked, terms
):
    small = [
        pltpu.make_async_copy(a, b, more.at[i])
        for i, (a, b) in enumerate(((flow_in, flow_row), (link_in, link_row), (price_in, price)))
    ]

    def copy(g):
        rows = pl.ds(g * FETCH, FETCH)
        return pltpu.make_async_copy(tiles.at[rows], kept.at[rows], sems.at[g])

    for c in small:
        c.start()
    for g in range(S // FETCH):
        copy(g).start(priority=min(g, 1))
    for c in small:
        c.wait()
    used = count[0, 0]
    flow_used = used_index(flow_row[...], used)
    index[:S, :] = own_column(flow_row[...], used)
    column = own_column(link_row[...], used)
    index[S : 2 * S, :] = column
    index[2 * S : 2 * S + 1, :] = flow_used
    index[2 * S + 1 : 2 * S + 2, :] = used_index(link_row[...], used)
    at = lax.broadcasted_iota(jnp.int32, (S, T), 1)
    hits = [jnp.where(column == at + c * T, 1.0, 0.0).astype(bf16) for c in range(price.shape[0] // T)]
    picked[...] = dot(jnp.concatenate(hits, axis=1), price[...].astype(bf16)).astype(bf16)

    def ready(g):
        if g * GROUP % FETCH == 0:
            copy(g * GROUP // FETCH).wait()

    tile_terms(kept, ready, picked, terms)
    put_payload(out, terms[...], flow_used)


def early_kernel(index, *rest):
    blocks, out = rest[:-1], rest[-1]
    out[...] = matched_sum(index[:S, :], blocks, decode(blocks))


def early_price_kernel(*rest):
    blocks, (out, code, hits) = rest[:-3], rest[-3:]

    def emit(rows, total):
        out[rows, :] = total

    every_sum(blocks, code, hits, out.shape[0] // T, emit)


def load_kernel(index, own, tiles, early, *rest):
    blocks, (out, sent, terms) = rest[:-3], rest[-3:]
    route_sum = early[...] + matched_sum(index[:S, :], blocks, decode(blocks))
    sent[...] = (own[0] / (own[1] + route_sum)).astype(bf16)
    tile_terms(tiles, lambda g: None, sent, terms)
    put_payload(out, terms[...], index[2 * S + 1 : 2 * S + 2, :])


def route_kernel(index, own, tiles, *rest):
    blocks, (out, picked, terms) = rest[:-3], rest[-3:]
    load = matched_sum(index[S : 2 * S, :], blocks, decode(blocks))
    picked[...] = (own[2] * jnp.exp(step_size * (load / own[3] - 1.0))).astype(bf16)
    tile_terms(tiles, lambda g: None, picked, terms)
    put_payload(out, terms[...], index[2 * S : 2 * S + 1, :])


def every_sum(blocks, code, hits, n, emit):
    code[...] = decode(blocks)
    rows = lax.broadcasted_iota(jnp.int32, (S, T), 0)
    chunk, scale = [], []
    for ref in blocks:
        for k in range(PIECES):
            index, factor = index_and_scale(ref, k)
            at = slice(len(chunk) * T, (len(chunk) + 1) * T)
            hits[:, at] = jnp.where(rows == (index & (T - 1)), 1.0, 0.0).astype(bf16)
            chunk.append(index >> 7)
            scale.append(factor)
    chunk = jnp.concatenate(chunk, axis=1)
    scale = jnp.concatenate(scale, axis=1)
    for c in range(n):
        mine = jnp.where(chunk == c, scale, 0.0)
        mine = jnp.broadcast_to(mine, (GROUP, mine.shape[1])).astype(bf16)
        both = dot(hits[...] * jnp.concatenate([mine] * (S // GROUP), axis=0), code[...])
        emit(slice(c * T, (c + 1) * T), both[:, :T] + both[:, T:])


def rate_kernel(weight, access, *rest):
    blocks, (out, code, hits) = rest[:-3], rest[-3:]

    def emit(rows, total):
        out[rows, :] = weight[rows, :] / (access[rows, :] + total)

    every_sum(blocks, code, hits, out.shape[0] // T, emit)


def first_price_kernel(price, capacity, *rest):
    blocks, (out, code, hits) = rest[:-3], rest[-3:]

    def emit(rows, total):
        out[rows, :] = price[rows, :] * jnp.exp(step_size * (total / capacity[rows, :] - 1.0))

    every_sum(blocks, code, hits, out.shape[0] // T, emit)


def last_price_kernel(price, capacity, early, rate, *rest):
    blocks, (out, rate_out, code, hits, buf, sems) = rest[:-6], rest[-6:]
    copies = [pltpu.make_async_copy(rate, rate_out, sems.at[0])]
    copies[0].start()

    def emit(rows, total):
        buf[rows, :] = price[rows, :] * jnp.exp(step_size * ((early[rows, :] + total) / capacity[rows, :] - 1.0))
        copies.append(pltpu.make_async_copy(buf.at[rows], out.at[rows], sems.at[len(copies)]))
        copies[-1].start()

    every_sum(blocks, code, hits, out.shape[0] // T, emit)
    for c in copies:
        c.wait()


def look_up(classes, table, weight):
    low = jnp.broadcast_to(table[0:1, :], (8, T))
    high = jnp.broadcast_to(table[1:2, :], (8, T))

    def look(r, carry):
        rows = pl.ds(pl.multiple_of(r * 8, 8), 8)
        which = classes[rows, :]
        lane = which & (T - 1)
        from_low = jnp.take_along_axis(low, lane, axis=1)
        from_high = jnp.take_along_axis(high, lane, axis=1)
        weight[rows, :] = jnp.where(which < T, from_low, from_high)
        return carry

    lax.fori_loop(0, classes.shape[0] // 8, look, 0, unroll=16)


def weigh_kernel(flow_class, table, weight):
    look_up(flow_class, table, weight)


def prepare_kernel(flow_at, link_at, flow_class, table, access, price, capacity, own, own_class):
    def pick(s, carry):
        f = flow_at[0, s]
        l = link_at[0, s]
        own_class[pl.ds(s, 1), :] = flow_class[pl.ds(f, 1), :]
        own[1, pl.ds(s, 1), :] = access[pl.ds(f, 1), :]
        own[2, pl.ds(s, 1), :] = price[pl.ds(l, 1), :]
        own[3, pl.ds(s, 1), :] = capacity[pl.ds(l, 1), :]
        return carry

    lax.fori_loop(0, S, pick, 0, unroll=16)
    look_up(own_class, table, own.at[0])


def shifts():
    def device(y, core, x, z):
        return ((y % 4) * 2 + core) * 16 + (x % 4) * 4 + z % 4

    every = [(y, c, x, z) for y in range(4) for c in range(2) for x in range(4) for z in range(4)]

    def moved(f):
        return [(device(*p), device(*f(*p))) for p in every]

    order = (1, 3, 2)
    first = [moved(lambda y, c, x, z, d=d: (y, 1, x + d, z) if c == 0 else (y, 0, x, z + d)) for d in order]
    second = [moved(lambda y, c, x, z, d=d: (y, 1, x + d, z) if c == 0 else (y, 0, x, z + d)) for d in order]
    along_y = [moved(lambda y, c, x, z, d=d: (y + d, 1 - c, x, z)) for d in order]
    partner = moved(lambda y, c, x, z: (y, 1 - c, x, z))
    return first, second, along_y, partner


FIRST, SECOND, ALONG_Y, PARTNER = shifts()


def send(x, perm):
    return lax.ppermute(x, ("flow", "link"), perm)


def gather_link(x):
    near, far = [send(x, PARTNER)], []
    for p in FIRST:
        near.append(send(x, p))
    near = gathered(near)
    for p in SECOND:
        far.append(send(near, p))
    return [send(near, PARTNER)] + far


def gather_flow(x):
    near = [x]
    for p in ALONG_Y:
        near.append(send(x, p))
    near = gathered(near)
    return [near, send(near, PARTNER)]


def on_device(
    route_tiles,
    tile_count,
    tile_flow,
    tile_link,
    flow_class,
    class_weight,
    access_price,
    capacity,
    init_price,
):
    flow_blocks = access_price.shape[0] // T
    link_blocks = capacity.shape[0] // T
    cap = capacity.reshape(link_blocks, T)
    price = init_price.reshape(link_blocks, T)
    access = access_price.reshape(flow_blocks, T)
    payload = pltpu.VMEM((PAYLOAD, T), jnp.int32)

    def early_call(blocks):
        return pl.pallas_call(
            early_kernel,
            out_shape=pltpu.VMEM((S, T), f32),
            in_specs=[VM] * (1 + len(blocks)),
            out_specs=VM,
            compiler_params=PARAMS,
        )(in_vmem(index), *[in_vmem(x) for x in blocks])

    def load_call(routes):
        early = early_call([routes[0]] + routes[2:])
        return tile_call(load_kernel, own, turned, [early], [routes[1]])

    def tile_call(body, own, tiles, early, blocks):
        return pl.pallas_call(
            body,
            out_shape=payload,
            in_specs=[VM] * (3 + len(early) + len(blocks)),
            out_specs=VM,
            scratch_shapes=[pltpu.VMEM((S, T), bf16), pltpu.VMEM((S, T), f32)],
            compiler_params=PARAMS,
        )(in_vmem(index), in_vmem(own), in_vmem(tiles), *[in_vmem(x) for x in early + blocks])

    def early_price_call(blocks):
        pieces = PIECES * len(blocks)
        return pl.pallas_call(
            early_price_kernel,
            out_shape=pltpu.VMEM(price.shape, f32),
            in_specs=[VM] * len(blocks),
            out_specs=VM,
            scratch_shapes=[pltpu.VMEM((pieces * S, 2 * T), bf16), pltpu.VMEM((S, pieces * S), bf16)],
            compiler_params=PARAMS,
        )(*[in_vmem(x) for x in blocks])

    def full_call(body, a, b, early, blocks, last):
        pieces = PIECES * len(blocks)
        scratch = [pltpu.VMEM((pieces * S, 2 * T), bf16), pltpu.VMEM((S, pieces * S), bf16)]
        if last:
            scratch += [pltpu.VMEM(a.shape, f32), pltpu.SemaphoreType.DMA((1 + a.shape[0] // T,))]
        return pl.pallas_call(
            body,
            out_shape=tuple(pltpu.HBM(x.shape, f32) for x in (a, early[1])) if last else pltpu.VMEM(a.shape, f32),
            in_specs=[VM] * (2 + len(early) + len(blocks)),
            out_specs=(HB, HB) if last else VM,
            scratch_shapes=scratch,
            compiler_params=PARAMS,
        )(in_vmem(a), in_vmem(b), *[in_vmem(x) for x in early + blocks])

    route_one, tiles, index = pl.pallas_call(
        first_route_kernel,
        out_shape=(payload, pltpu.VMEM((S, T, T), bf16), pltpu.VMEM((2 * S + 8, T), jnp.int32)),
        in_specs=[SM] + [HB] * 4,
        out_specs=(VM, VM, VM),
        scratch_shapes=[
            pltpu.SemaphoreType.DMA((S // FETCH,)),
            pltpu.SemaphoreType.DMA((3,)),
            pltpu.VMEM((1, S), jnp.int32),
            pltpu.VMEM((1, S), jnp.int32),
            pltpu.VMEM(price.shape, f32),
            pltpu.VMEM((S, T), bf16),
            pltpu.VMEM((S, T), f32),
        ],
        compiler_params=PARAMS,
        name="first_route",
    )(tile_count, *[in_hbm(x) for x in (tile_flow, tile_link, price, route_tiles)])
    fetched = (
        pltpu.SMEM((1, S), jnp.int32),
        pltpu.SMEM((1, S), jnp.int32),
        pltpu.VMEM((flow_blocks, T), jnp.int32),
        pltpu.VMEM((2, T), f32),
        pltpu.VMEM(access.shape, f32),
        pltpu.VMEM(price.shape, f32),
        pltpu.VMEM(cap.shape, f32),
    )
    sources = (tile_flow, tile_link, flow_class.reshape(flow_blocks, T), class_weight.reshape(2, T), access, price, cap)
    turned, flow_at, link_at, *sources = pl.pallas_call(
        turn_kernel,
        out_shape=(pltpu.VMEM((S, T, T), bf16), *fetched),
        in_specs=[VM] + [HB] * 7,
        out_specs=(VM, SM, SM) + (VM,) * 5,
        scratch_shapes=[pltpu.SemaphoreType.DMA((7,))],
        compiler_params=PARAMS,
        name="turn",
    )(in_vmem(tiles), *[in_hbm(x) for x in sources])
    access, price, cap = sources[2:]
    weight = pl.pallas_call(
        weigh_kernel,
        out_shape=pltpu.VMEM((flow_blocks, T), f32),
        in_specs=[VM, VM],
        out_specs=VM,
        compiler_params=PARAMS,
        name="weigh",
    )(in_vmem(sources[0]), in_vmem(sources[1]))
    own = pl.pallas_call(
        prepare_kernel,
        out_shape=pltpu.VMEM((4, S, T), f32),
        in_specs=[SM, SM] + [VM] * 5,
        out_specs=VM,
        scratch_shapes=[pltpu.VMEM((S, T), jnp.int32)],
        compiler_params=PARAMS,
        name="prepare",
    )(flow_at, link_at, *[in_vmem(x) for x in sources])

    routes = gather_link(route_one)
    loads = gather_flow(load_call(routes))
    price_one = full_call(first_price_kernel, price, cap, [], loads, False)
    routes = gather_link(tile_call(route_kernel, own, tiles, [], loads))
    rate = full_call(rate_kernel, weight, access, [], routes, False)
    loads = gather_flow(load_call(routes))
    early = early_price_call(loads[:1])
    price_two, rate = full_call(last_price_kernel, price_one, cap, [early, rate], loads[1:], True)
    return (rate.reshape(-1), price_two.reshape(-1))


def solution(mesh):
    return jax.shard_map(
        on_device,
        mesh=mesh,
        in_specs=(
            P("flow", "link", None),
            P("flow", "link"),
            P("flow", "link"),
            P("flow", "link"),
            P("flow"),
            P(),
            P("flow"),
            P("link"),
            P("link"),
        ),
        out_specs=(P("flow"), P("link")),
        check_vma=False,
    )
```

```python
import jax
import jax.numpy as jnp
from jax import lax
from jax.experimental import pallas as pl
from jax.experimental.pallas import tpu as pltpu
from jax.sharding import PartitionSpec as P


step_size = 0.5


f32 = jnp.float32
bf16 = jnp.bfloat16

T = 128
S = 128
HALF = S // 2
PAYLOAD = HALF + 8
INDEX = HALF
EXPONENT = HALF + 1
PIECES = 4
GROUP = 16
CHUNKS = S // GROUP
FETCH = 64

SM = pl.BlockSpec(memory_space=pltpu.SMEM)
HB = pl.BlockSpec(memory_space=pltpu.HBM)
VM = pl.BlockSpec(memory_space=pltpu.VMEM)
PARAMS = pltpu.CompilerParams(vmem_limit_bytes=16 << 20)


def in_vmem(x):
    return pltpu.with_memory_space_constraint(x, pltpu.VMEM)


def in_hbm(x):
    return pltpu.with_memory_space_constraint(x, pltpu.HBM)


def dot(a, b):
    return lax.dot_general(a, b, (((1,), (0,)), ((), ())), preferred_element_type=f32)


def used_index(index_row, count, unused=-1):
    slot = lax.broadcasted_iota(jnp.int32, index_row.shape, 1)
    return jnp.where(slot < count, index_row, unused)


def own_column(index_row, count):
    row = used_index(index_row, count, -2).astype(f32)
    return jnp.broadcast_to(row, (S, S)).T.astype(jnp.int32)


def put_payload(out, terms, index_row):
    largest = jnp.max(terms, axis=1, keepdims=True)
    exponent = jnp.floor(jnp.log(jnp.maximum(largest, 1e-30)) * 1.4426950408889634) + 1.0
    scale = jnp.exp2(16.0 - exponent)
    coded = jnp.minimum(jnp.round(terms * scale), 65535.0).astype(jnp.int32)
    out[:HALF, :] = coded[:HALF, :] | (coded[HALF:, :] << 16)
    out[INDEX:EXPONENT, :] = index_row
    exponent_row = jnp.broadcast_to(exponent, (S, S)).T[:1, :].astype(jnp.int32)
    out[EXPONENT : EXPONENT + 1, :] = exponent_row


def decoded(words):
    top = lax.shift_right_logical(words, 16)
    high = jnp.concatenate([words & 0xFF00, top & 0xFF00], axis=0)
    low = jnp.concatenate([words & 0xFF, top & 0xFF], axis=0)
    return jnp.concatenate([high.astype(f32).astype(bf16), low.astype(f32).astype(bf16)], axis=1)


def matched_sum(column, blocks, codes):
    hits = []
    for ref in blocks:
        for k in range(PIECES):
            index, scale = index_and_scale(ref, k)
            hits.append(jnp.where(column == index, scale, 0.0).astype(bf16))
    both = dot(jnp.concatenate(hits, axis=1), codes)
    return both[:, :T] + both[:, T:]


def decode(blocks):
    words = [ref[k * HALF : (k + 1) * HALF, :] for ref in blocks for k in range(PIECES)]
    return jnp.concatenate([decoded(w) for w in words], axis=0)


def index_and_scale(ref, k):
    at = PIECES * HALF + 2 * k
    return ref[at : at + 1, :], jnp.exp2((ref[at + 1 : at + 2, :] - 16).astype(f32))


def join_kernel(*refs):
    payloads, out = refs[:-1], refs[-1]
    for k, p in enumerate(payloads):
        out[k * HALF : (k + 1) * HALF, :] = p[:HALF, :]
        at = PIECES * HALF + 2 * k
        out[at : at + 2, :] = p[INDEX : EXPONENT + 1, :]


def gathered(payloads):
    return pl.pallas_call(
        join_kernel,
        out_shape=pltpu.VMEM((PIECES * HALF + 2 * PIECES, T), jnp.int32),
        in_specs=[VM] * PIECES,
        out_specs=VM,
        compiler_params=PARAMS,
        name="join",
    )(*[in_vmem(p) for p in payloads])


def own_slots():
    lane_slot = lax.broadcasted_iota(jnp.int32, (GROUP, GROUP * T), 1) // T
    return lane_slot == lax.broadcasted_iota(jnp.int32, (GROUP, GROUP * T), 0)


def spread(rows, own):
    return jnp.where(own, jnp.concatenate([rows] * GROUP, axis=1).astype(f32), 0.0).astype(bf16)


def tile_terms(tiles, ready, picked, out):
    own = own_slots()
    for g in range(CHUNKS):
        ready(g)
        rows = slice(g * GROUP, (g + 1) * GROUP)
        out[rows, :] = dot(spread(picked[rows, :], own), tiles[rows].reshape(GROUP * T, T))


def turn_kernel(tiles, *rest):
    sources, (out, *kept), sems = rest[:7], rest[7:15], rest[15]
    copies = [pltpu.make_async_copy(a, b, sems.at[i]) for i, (a, b) in enumerate(zip(sources, kept))]
    for c in copies:
        c.start()
    for s in range(S):
        out[s] = tiles[s].T
    for c in copies:
        c.wait()


def first_route_kernel(
    count, flow_in, link_in, price_in, tiles, out, kept, index, sems, more, flow_row, link_row, price, picked, terms
):
    small = [
        pltpu.make_async_copy(a, b, more.at[i])
        for i, (a, b) in enumerate(((flow_in, flow_row), (link_in, link_row), (price_in, price)))
    ]

    def copy(g):
        rows = pl.ds(g * FETCH, FETCH)
        return pltpu.make_async_copy(tiles.at[rows], kept.at[rows], sems.at[g])

    for c in small:
        c.start()
    for g in range(S // FETCH):
        copy(g).start(priority=min(g, 1))
    for c in small:
        c.wait()
    used = count[0, 0]
    flow_used = used_index(flow_row[...], used)
    index[:S, :] = own_column(flow_row[...], used)
    column = own_column(link_row[...], used)
    index[S : 2 * S, :] = column
    index[2 * S : 2 * S + 1, :] = flow_used
    index[2 * S + 1 : 2 * S + 2, :] = used_index(link_row[...], used)
    at = lax.broadcasted_iota(jnp.int32, (S, T), 1)
    hits = [jnp.where(column == at + c * T, 1.0, 0.0).astype(bf16) for c in range(price.shape[0] // T)]
    picked[...] = dot(jnp.concatenate(hits, axis=1), price[...].astype(bf16)).astype(bf16)

    def ready(g):
        if g * GROUP % FETCH == 0:
            copy(g * GROUP // FETCH).wait()

    tile_terms(kept, ready, picked, terms)
    put_payload(out, terms[...], flow_used)


def early_kernel(index, *rest):
    blocks, out = rest[:-1], rest[-1]
    out[...] = matched_sum(index[:S, :], blocks, decode(blocks))


def early_load_kernel(index, *rest):
    blocks, out = rest[:-1], rest[-1]
    out[...] = matched_sum(index[S : 2 * S, :], blocks, decode(blocks))


def early_price_kernel(*rest):
    blocks, (out, code, hits) = rest[:-3], rest[-3:]

    def emit(rows, total):
        out[rows, :] = total

    every_sum(blocks, code, hits, out.shape[0] // T, emit)


def load_kernel(index, own, tiles, early, *rest):
    blocks, (out, sent, terms) = rest[:-3], rest[-3:]
    route_sum = early[...] + matched_sum(index[:S, :], blocks, decode(blocks))
    sent[...] = (own[0] / (own[1] + route_sum)).astype(bf16)
    tile_terms(tiles, lambda g: None, sent, terms)
    put_payload(out, terms[...], index[2 * S + 1 : 2 * S + 2, :])


def route_kernel(index, own, tiles, early, *rest):
    blocks, (out, picked, terms) = rest[:-3], rest[-3:]
    load = early[...] + matched_sum(index[S : 2 * S, :], blocks, decode(blocks))
    picked[...] = (own[2] * jnp.exp(step_size * (load / own[3] - 1.0))).astype(bf16)
    tile_terms(tiles, lambda g: None, picked, terms)
    put_payload(out, terms[...], index[2 * S : 2 * S + 1, :])


def every_sum(blocks, code, hits, n, emit):
    code[...] = decode(blocks)
    rows = lax.broadcasted_iota(jnp.int32, (S, T), 0)
    chunk, scale = [], []
    for ref in blocks:
        for k in range(PIECES):
            index, factor = index_and_scale(ref, k)
            at = slice(len(chunk) * T, (len(chunk) + 1) * T)
            hits[:, at] = jnp.where(rows == (index & (T - 1)), 1.0, 0.0).astype(bf16)
            chunk.append(index >> 7)
            scale.append(factor)
    chunk = jnp.concatenate(chunk, axis=1)
    scale = jnp.concatenate(scale, axis=1)
    for c in range(n):
        mine = jnp.where(chunk == c, scale, 0.0)
        mine = jnp.broadcast_to(mine, (GROUP, mine.shape[1])).astype(bf16)
        both = dot(hits[...] * jnp.concatenate([mine] * (S // GROUP), axis=0), code[...])
        emit(slice(c * T, (c + 1) * T), both[:, :T] + both[:, T:])


def rate_kernel(weight, access, *rest):
    blocks, (out, code, hits) = rest[:-3], rest[-3:]

    def emit(rows, total):
        out[rows, :] = weight[rows, :] / (access[rows, :] + total)

    every_sum(blocks, code, hits, out.shape[0] // T, emit)


def first_price_kernel(price, capacity, *rest):
    blocks, (out, code, hits) = rest[:-3], rest[-3:]

    def emit(rows, total):
        out[rows, :] = price[rows, :] * jnp.exp(step_size * (total / capacity[rows, :] - 1.0))

    every_sum(blocks, code, hits, out.shape[0] // T, emit)


def last_price_kernel(price, capacity, early, rate, *rest):
    blocks, (out, rate_out, code, hits, buf, sems) = rest[:-6], rest[-6:]
    copies = [pltpu.make_async_copy(rate, rate_out, sems.at[0])]
    copies[0].start()

    def emit(rows, total):
        buf[rows, :] = price[rows, :] * jnp.exp(step_size * ((early[rows, :] + total) / capacity[rows, :] - 1.0))
        copies.append(pltpu.make_async_copy(buf.at[rows], out.at[rows], sems.at[len(copies)]))
        copies[-1].start()

    every_sum(blocks, code, hits, out.shape[0] // T, emit)
    for c in copies:
        c.wait()


def look_up(classes, table, weight):
    low = jnp.broadcast_to(table[0:1, :], (8, T))
    high = jnp.broadcast_to(table[1:2, :], (8, T))

    def look(r, carry):
        rows = pl.ds(pl.multiple_of(r * 8, 8), 8)
        which = classes[rows, :]
        lane = which & (T - 1)
        from_low = jnp.take_along_axis(low, lane, axis=1)
        from_high = jnp.take_along_axis(high, lane, axis=1)
        weight[rows, :] = jnp.where(which < T, from_low, from_high)
        return carry

    lax.fori_loop(0, classes.shape[0] // 8, look, 0, unroll=16)


def weigh_kernel(flow_class, table, weight):
    look_up(flow_class, table, weight)


def prepare_kernel(flow_at, link_at, flow_class, table, access, price, capacity, own, own_class):
    def pick(s, carry):
        f = flow_at[0, s]
        l = link_at[0, s]
        own_class[pl.ds(s, 1), :] = flow_class[pl.ds(f, 1), :]
        own[1, pl.ds(s, 1), :] = access[pl.ds(f, 1), :]
        own[2, pl.ds(s, 1), :] = price[pl.ds(l, 1), :]
        own[3, pl.ds(s, 1), :] = capacity[pl.ds(l, 1), :]
        return carry

    lax.fori_loop(0, S, pick, 0, unroll=16)
    look_up(own_class, table, own.at[0])


def shifts():
    def device(y, core, x, z):
        return ((y % 4) * 2 + core) * 16 + (x % 4) * 4 + z % 4

    every = [(y, c, x, z) for y in range(4) for c in range(2) for x in range(4) for z in range(4)]

    def moved(f):
        return [(device(*p), device(*f(*p))) for p in every]

    order = (1, 3, 2)
    first = [moved(lambda y, c, x, z, d=d: (y, 1, x + d, z) if c == 0 else (y, 0, x, z + d)) for d in order]
    second = [moved(lambda y, c, x, z, d=d: (y, 1, x + d, z) if c == 0 else (y, 0, x, z + d)) for d in order]
    along_y = [moved(lambda y, c, x, z, d=d: (y + d, 1 - c, x, z)) for d in order]
    partner = moved(lambda y, c, x, z: (y, 1 - c, x, z))
    return first, second, along_y, partner


FIRST, SECOND, ALONG_Y, PARTNER = shifts()


def send(x, perm):
    return lax.ppermute(x, ("flow", "link"), perm)


def gather_link(x):
    near, far = [send(x, PARTNER)], []
    for p in FIRST:
        near.append(send(x, p))
    near = gathered(near)
    for p in SECOND:
        far.append(send(near, p))
    return [send(near, PARTNER)] + far


def gather_flow(x):
    near = [x]
    for p in ALONG_Y:
        near.append(send(x, p))
    near = gathered(near)
    return [near, send(near, PARTNER)]


def on_device(
    route_tiles,
    tile_count,
    tile_flow,
    tile_link,
    flow_class,
    class_weight,
    access_price,
    capacity,
    init_price,
):
    flow_blocks = access_price.shape[0] // T
    link_blocks = capacity.shape[0] // T
    cap = capacity.reshape(link_blocks, T)
    price = init_price.reshape(link_blocks, T)
    access = access_price.reshape(flow_blocks, T)
    payload = pltpu.VMEM((PAYLOAD, T), jnp.int32)

    def early_call(blocks, body=early_kernel):
        return pl.pallas_call(
            body,
            out_shape=pltpu.VMEM((S, T), f32),
            in_specs=[VM] * (1 + len(blocks)),
            out_specs=VM,
            compiler_params=PARAMS,
        )(in_vmem(index), *[in_vmem(x) for x in blocks])

    def load_call(routes):
        early = early_call([routes[0]] + routes[2:])
        return tile_call(load_kernel, own, turned, [early], [routes[1]])

    def route_call(loads):
        early = early_call(loads[:1], early_load_kernel)
        return tile_call(route_kernel, own, tiles, [early], loads[1:])

    def tile_call(body, own, tiles, early, blocks):
        return pl.pallas_call(
            body,
            out_shape=payload,
            in_specs=[VM] * (3 + len(early) + len(blocks)),
            out_specs=VM,
            scratch_shapes=[pltpu.VMEM((S, T), bf16), pltpu.VMEM((S, T), f32)],
            compiler_params=PARAMS,
        )(in_vmem(index), in_vmem(own), in_vmem(tiles), *[in_vmem(x) for x in early + blocks])

    def early_price_call(blocks):
        pieces = PIECES * len(blocks)
        return pl.pallas_call(
            early_price_kernel,
            out_shape=pltpu.VMEM(price.shape, f32),
            in_specs=[VM] * len(blocks),
            out_specs=VM,
            scratch_shapes=[pltpu.VMEM((pieces * S, 2 * T), bf16), pltpu.VMEM((S, pieces * S), bf16)],
            compiler_params=PARAMS,
        )(*[in_vmem(x) for x in blocks])

    def full_call(body, a, b, early, blocks, last):
        pieces = PIECES * len(blocks)
        scratch = [pltpu.VMEM((pieces * S, 2 * T), bf16), pltpu.VMEM((S, pieces * S), bf16)]
        if last:
            scratch += [pltpu.VMEM(a.shape, f32), pltpu.SemaphoreType.DMA((1 + a.shape[0] // T,))]
        return pl.pallas_call(
            body,
            out_shape=tuple(pltpu.HBM(x.shape, f32) for x in (a, early[1])) if last else pltpu.VMEM(a.shape, f32),
            in_specs=[VM] * (2 + len(early) + len(blocks)),
            out_specs=(HB, HB) if last else VM,
            scratch_shapes=scratch,
            compiler_params=PARAMS,
        )(in_vmem(a), in_vmem(b), *[in_vmem(x) for x in early + blocks])

    route_one, tiles, index = pl.pallas_call(
        first_route_kernel,
        out_shape=(payload, pltpu.VMEM((S, T, T), bf16), pltpu.VMEM((2 * S + 8, T), jnp.int32)),
        in_specs=[SM] + [HB] * 4,
        out_specs=(VM, VM, VM),
        scratch_shapes=[
            pltpu.SemaphoreType.DMA((S // FETCH,)),
            pltpu.SemaphoreType.DMA((3,)),
            pltpu.VMEM((1, S), jnp.int32),
            pltpu.VMEM((1, S), jnp.int32),
            pltpu.VMEM(price.shape, f32),
            pltpu.VMEM((S, T), bf16),
            pltpu.VMEM((S, T), f32),
        ],
        compiler_params=PARAMS,
        name="first_route",
    )(tile_count, *[in_hbm(x) for x in (tile_flow, tile_link, price, route_tiles)])
    fetched = (
        pltpu.SMEM((1, S), jnp.int32),
        pltpu.SMEM((1, S), jnp.int32),
        pltpu.VMEM((flow_blocks, T), jnp.int32),
        pltpu.VMEM((2, T), f32),
        pltpu.VMEM(access.shape, f32),
        pltpu.VMEM(price.shape, f32),
        pltpu.VMEM(cap.shape, f32),
    )
    sources = (tile_flow, tile_link, flow_class.reshape(flow_blocks, T), class_weight.reshape(2, T), access, price, cap)
    turned, flow_at, link_at, *sources = pl.pallas_call(
        turn_kernel,
        out_shape=(pltpu.VMEM((S, T, T), bf16), *fetched),
        in_specs=[VM] + [HB] * 7,
        out_specs=(VM, SM, SM) + (VM,) * 5,
        scratch_shapes=[pltpu.SemaphoreType.DMA((7,))],
        compiler_params=PARAMS,
        name="turn",
    )(in_vmem(tiles), *[in_hbm(x) for x in sources])
    access, price, cap = sources[2:]
    weight = pl.pallas_call(
        weigh_kernel,
        out_shape=pltpu.VMEM((flow_blocks, T), f32),
        in_specs=[VM, VM],
        out_specs=VM,
        compiler_params=PARAMS,
        name="weigh",
    )(in_vmem(sources[0]), in_vmem(sources[1]))
    own = pl.pallas_call(
        prepare_kernel,
        out_shape=pltpu.VMEM((4, S, T), f32),
        in_specs=[SM, SM] + [VM] * 5,
        out_specs=VM,
        scratch_shapes=[pltpu.VMEM((S, T), jnp.int32)],
        compiler_params=PARAMS,
        name="prepare",
    )(flow_at, link_at, *[in_vmem(x) for x in sources])

    routes = gather_link(route_one)
    loads = gather_flow(load_call(routes))
    price_one = full_call(first_price_kernel, price, cap, [], loads, False)
    routes = gather_link(route_call(loads))
    rate = full_call(rate_kernel, weight, access, [], routes, False)
    loads = gather_flow(load_call(routes))
    early = early_price_call(loads[:1])
    price_two, rate = full_call(last_price_kernel, price_one, cap, [early, rate], loads[1:], True)
    return (rate.reshape(-1), price_two.reshape(-1))


def solution(mesh):
    return jax.shard_map(
        on_device,
        mesh=mesh,
        in_specs=(
            P("flow", "link", None),
            P("flow", "link"),
            P("flow", "link"),
            P("flow", "link"),
            P("flow"),
            P(),
            P("flow"),
            P("link"),
            P("link"),
        ),
        out_specs=(P("flow"), P("link")),
        check_vma=False,
    )
```
